128 devices in a mesh: seq: 32 (over y, x, core), head: 4 (over z).
Axes of the slice: x: 4, y: 4, z: 4, core: 2. Of those that a mesh axis runs over, the one named last changes fastest.
Arguments:
- queries: float32 [32768, 8192], P('seq', 'head'), may hold values from -200 to 200, as said below
- keys: float32 [32768, 1024], P('seq', 'head'), may hold values from -8 to 8, as said below
- values: float32 [32768, 1024], P('seq', 'head'), may hold values from -40 to 40, as said below
- gain: float32 [8192], P('head'), may hold values from 0.1 to 1.9
Outputs:
- attended: float32 [32768, 8192], P('seq', 'head')
The draws below stay inside these ranges and needn't reach their ends.
Inputs may be any that keep to these rules, and one draw needn't show every extreme that they name: `queries`: queries are real-valued. `keys`: keys are real-valued of order one. `values`: values are real-valued; their scale differs between heads.
All inputs are finite; a program needn't handle non-finite values.
Results may differ from the reference program's by a relative error of at most 0.0003.
Values sent between devices are 32-bit elements; how exact they have to be, the bound alone decides.
No kernel may reach another device: no remote copies, remote signals or barrier semaphores. Data moves between devices by JAX's collectives and lax.ppermute only.
A program may use at most 128 MiB of HBM per device.

```python
import math
import jax
import jax.numpy as jnp
from jax import lax

QUERY_HEADS = 64
KEY_VALUE_HEADS = 8
HEAD_DIMENSION = 128
WINDOW = 128
DOCUMENT_TOKENS = 32768


def shared_keys(key):
    base_offset = jnp.clip(jax.random.normal(jax.random.fold_in(key, 11), (DOCUMENT_TOKENS, KEY_VALUE_HEADS, HEAD_DIMENSION), jnp.float32), -6.0, 6.0)
    return base_offset


def draw_keys(key, part):
    base_offset = shared_keys(key)
    return base_offset.reshape(DOCUMENT_TOKENS, KEY_VALUE_HEADS * HEAD_DIMENSION)


def draw_queries(key, part):
    drawn_softmax = jnp.clip(jax.random.normal(jax.random.fold_in(key, 13), (DOCUMENT_TOKENS, KEY_VALUE_HEADS, QUERY_HEADS // KEY_VALUE_HEADS, HEAD_DIMENSION), jnp.float32), -6.0, 6.0)
    return drawn_softmax.reshape(DOCUMENT_TOKENS, QUERY_HEADS * HEAD_DIMENSION)


def draw_values(key, part):
    level_value = jnp.arange(KEY_VALUE_HEADS, dtype=jnp.float32) / max(KEY_VALUE_HEADS - 1, 1)
    small_perturbation = jnp.exp(jax.random.uniform(jax.random.fold_in(key, 21), (KEY_VALUE_HEADS,), jnp.float32, -0.1, 0.1))
    score_scale = 0.5 * 10.0 ** level_value * small_perturbation
    mixed_output = jnp.clip(jax.random.normal(jax.random.fold_in(key, 24), (DOCUMENT_TOKENS, KEY_VALUE_HEADS, HEAD_DIMENSION), jnp.float32), -6.0, 6.0)
    return (mixed_output * score_scale[None, :, None]).reshape(DOCUMENT_TOKENS, KEY_VALUE_HEADS * HEAD_DIMENSION)


def setup_inputs(seed: int = 0) -> dict:
    key_of = jax.random.split(jax.random.key(seed), 5)
    queries = draw_queries(jax.random.fold_in(key_of[4], 71), 0)
    keys = draw_keys(jax.random.fold_in(key_of[4], 71), 0)
    values = draw_values(jax.random.fold_in(key_of[4], 71), 0)
    gain = jnp.clip(1.0 + 0.18 * jax.random.normal(key_of[3], (QUERY_HEADS * HEAD_DIMENSION,), jnp.float32), 0.1, 1.9)
    return dict(queries=queries, keys=keys, values=values, gain=gain)


HIGH_ACCURACY = lax.Precision.HIGHEST

def reference(queries, keys, values, gain):
    block_index = math.gcd(DOCUMENT_TOKENS, 128)
    block_count = DOCUMENT_TOKENS // block_index
    group_count = QUERY_HEADS // KEY_VALUE_HEADS
    window_border = WINDOW - 1
    query_tensor = queries.reshape(block_count, block_index, KEY_VALUE_HEADS, group_count, HEAD_DIMENSION)
    key_tensor = keys.reshape(block_count, block_index, KEY_VALUE_HEADS, HEAD_DIMENSION)
    value_tensor = values.reshape(block_count, block_index, KEY_VALUE_HEADS, HEAD_DIMENSION)
    score_scale = 1.0 / math.sqrt(HEAD_DIMENSION)
    rows = jnp.arange(block_index, dtype=jnp.int32)
    cols = jnp.arange(window_border + block_index, dtype=jnp.int32)

    def advance(carry, inputs):
        state, prev_k, prev_v = carry
        query_block, key_block, value_block, number = inputs
        query_features = jnp.tanh(query_block)
        key_features = jnp.tanh(key_block)
        causal = rows[:, None] >= rows[None, :]
        inner_product = jnp.einsum('cmop,nmp->mocn', query_features, key_features, precision=HIGH_ACCURACY)
        inner_product = jnp.where(causal[None, None], inner_product, 0.0)
        linear_branch = jnp.einsum('xjpa,axf->pxjf', inner_product, value_block, precision=HIGH_ACCURACY)
        linear_branch = linear_branch + jnp.einsum('tgrd,gde->tgre', query_features, state, precision=HIGH_ACCURACY)
        state = state + jnp.einsum('sgd,sge->gde', key_features, value_block, precision=HIGH_ACCURACY)
        every_key_row = jnp.concatenate([prev_k, key_block], 0)
        every_value_row = jnp.concatenate([prev_v, value_block], 0)
        q_pos = number * block_index + rows
        k_pos = number * block_index - window_border + cols
        valid = (k_pos[None, :] <= q_pos[:, None]) & (k_pos[None, :] > q_pos[:, None] - WINDOW) & (k_pos[None, :] >= 0)
        score_matrix = jnp.einsum('cmop,nmp->mocn', query_block, every_key_row, precision=HIGH_ACCURACY) * score_scale
        score_matrix = jnp.where(valid[None, None], score_matrix, -jnp.inf)
        top = lax.optimization_barrier(jnp.max(score_matrix, axis=3, keepdims=True))
        softmax_weights = jnp.where(valid[None, None], jnp.exp(score_matrix - top), 0.0)
        total = lax.optimization_barrier(jnp.sum(softmax_weights, axis=3))
        window_length = jnp.einsum('xjpa,axf->pxjf', softmax_weights, every_value_row, precision=HIGH_ACCURACY)
        window_length = window_length / jnp.transpose(total, (2, 0, 1))[..., None]
        prev_k = every_key_row[block_index:]
        prev_v = every_value_row[block_index:]
        return ((state, prev_k, prev_v), (linear_branch, window_length))
    start_position = (jnp.zeros((KEY_VALUE_HEADS, HEAD_DIMENSION, HEAD_DIMENSION), jnp.float32), jnp.zeros((window_border, KEY_VALUE_HEADS, HEAD_DIMENSION), jnp.float32), jnp.zeros((window_border, KEY_VALUE_HEADS, HEAD_DIMENSION), jnp.float32))
    numbers = jnp.arange(block_count, dtype=jnp.int32)
    _, (linear_branch, window_length) = lax.scan(advance, start_position, (query_tensor, key_tensor, value_tensor, numbers))
    linear_branch = linear_branch.reshape(DOCUMENT_TOKENS, QUERY_HEADS * HEAD_DIMENSION)
    window_length = window_length.reshape(DOCUMENT_TOKENS, QUERY_HEADS * HEAD_DIMENSION)
    mean_sq = lax.optimization_barrier(jnp.mean(linear_branch * linear_branch, axis=1, keepdims=True))
    normed = linear_branch / jnp.sqrt(mean_sq + 1e-06) * gain[None, :]
    return normed + window_length
```

```python
import math

import jax
import jax.numpy as jnp
from jax import lax
from jax.experimental import pallas as pl
from jax.experimental.pallas import tpu as pltpu
from jax.sharding import PartitionSpec as P

QUERY_HEADS = 64
KEY_VALUE_HEADS = 8
D = 128
G = QUERY_HEADS // KEY_VALUE_HEADS
BLOCK = 128
EPS = 1e-6
SCORE_SCALE = math.log2(math.e) / math.sqrt(D)

f32 = jnp.float32
bf = jnp.bfloat16
NT = (((1,), (1,)), ((), ()))
TN = (((0,), (0,)), ((), ()))


def split(x):
    hi = x.astype(bf)
    return hi, (x - hi.astype(f32)).astype(bf)


def lanes(*xs):
    return jnp.concatenate(xs, axis=1)


def rows(*xs):
    return jnp.concatenate(xs, axis=0)


def dot(a, b, dims=(((1,), (0,)), ((), ()))):
    return lax.dot_general(a, b, dims, preferred_element_type=f32)


def halves(x):
    return x[:, :D] + x[:, D:]


def params(mib):
    return pltpu.CompilerParams(
        vmem_limit_bytes=mib << 20, dimension_semantics=("arbitrary", "arbitrary")
    )


def state_body(k_ref, v_ref, before_ref, total_ref):
    state = jnp.zeros((D, D), f32)
    for b in range(k_ref.shape[0] // BLOCK):
        at = slice(b * BLOCK, (b + 1) * BLOCK)
        before_ref[b] = state
        fh, fl = split(jnp.tanh(k_ref[at, :]))
        vh, vl = split(v_ref[at, :])
        vv = lanes(vh, vl)
        state = state + halves(dot(rows(fh, fl), rows(vv, vv), TN))
    total_ref[0] = state


def local_states(keys, values):
    count, width = keys.shape
    kv, nb = width // D, count // BLOCK
    return pl.pallas_call(
        state_body,
        grid=(kv, 1),
        in_specs=[pl.BlockSpec((count, D), lambda g, _: (0, g))] * 2,
        out_specs=[
            pl.BlockSpec((pl.Squeezed(), nb, D, D), lambda g, _: (g, 0, 0, 0)),
            pl.BlockSpec((1, D, D), lambda g, _: (g, 0, 0)),
        ],
        out_shape=[
            jax.ShapeDtypeStruct((kv, nb, D, D), f32),
            jax.ShapeDtypeStruct((kv, D, D), f32),
        ],
        compiler_params=params(5),
        name="local_states",
    )(keys, values)


def block_body(wrap, *refs):
    q_ref, k_ref, v_ref, kp_ref, vp_ref, *refs = refs
    if wrap is not None:
        kw_ref, vw_ref, *refs = refs
    win_ref, lin_ref, fq_ref, kh, kl, vv = refs
    b = pl.program_id(1)

    def prepare(k, v, at):
        h, l = split(k * SCORE_SCALE)
        kh[at, :] = lanes(h, h)
        kl[at, :] = lanes(l, l)
        vv[at, :] = lanes(*split(v))

    here = slice(0, BLOCK)
    there = slice(BLOCK, 2 * BLOCK)

    @pl.when(b == 0)
    def _():
        prepare(kp_ref[...], vp_ref[...], there)

    @pl.when(b > 0)
    def _():
        for x in (kh, kl, vv):
            x[there, :] = x[here, :]

    if wrap is not None:

        @pl.when(b == wrap)
        def _():
            prepare(kw_ref[...], vw_ref[...], there)

    k = k_ref[...]
    prepare(k, v_ref[...], here)
    fh, fl = split(jnp.tanh(k))
    ff = rows(lanes(fh, fh), lanes(fl, fl))
    kk = lanes(kh[...], kl[...])
    v_both = vv[...]
    v_own = vv[here, :]
    row = lax.broadcasted_iota(jnp.int32, (BLOCK, BLOCK), 0)
    col = lax.broadcasted_iota(jnp.int32, (BLOCK, BLOCK), 1)
    own = rows(*[row >= col] * G)
    zero = jnp.zeros((BLOCK * G, BLOCK), bf)

    q = rows(*[q_ref[:, i * D : (i + 1) * D] for i in range(G)])
    qh, ql = split(q)
    s = dot(lanes(qh, ql, qh, ql), kk, NT)
    f2 = lanes(*split(jnp.tanh(q)))
    for i in range(G):
        fq_ref[i] = f2[i * BLOCK : (i + 1) * BLOCK]
    a = jnp.where(own, halves(dot(f2, ff, NT)), 0.0)
    lin = halves(dot(lanes(*split(a)), rows(v_own, v_own)))
    before = s[:, BLOCK:]
    if wrap is not None:
        before = jnp.where((lax.axis_index("seq") > 0) | (b != wrap), before, -1e30)
    t = jnp.where(own, s[:, :BLOCK], before)
    p = jnp.exp2(t - jnp.max(t, axis=1, keepdims=True))
    total = jnp.sum(p, axis=1, keepdims=True)
    ph, pl_ = split(p)
    p4 = lanes(
        jnp.where(own, ph, zero),
        jnp.where(own, zero, ph),
        jnp.where(own, pl_, zero),
        jnp.where(own, zero, pl_),
    )
    win = halves(dot(p4, rows(v_both, v_both))) * (1.0 / total)
    for i in range(G):
        win_ref[:, i * D : (i + 1) * D] = win[i * BLOCK : (i + 1) * BLOCK]
        lin_ref[:, i * D : (i + 1) * D] = lin[i * BLOCK : (i + 1) * BLOCK]


def block_part(queries, keys, values, first, nb, wrap=None):
    count, width = queries.shape
    kv = keys.shape[1] // D
    total = count // BLOCK
    own = lambda g, b: ((first + b) % total, g)
    prior = lambda g, b: (first - 1, g)
    small = lambda index: pl.BlockSpec((BLOCK, D), index)
    args = [queries, keys, values, keys, values]
    specs = [pl.BlockSpec((BLOCK, G * D), own), small(own), small(own), small(prior), small(prior)]
    step = None
    if wrap is not None:
        step = total - first
        last = lambda g, b: (0, g)
        args += wrap
        specs += [small(last), small(last)]
    big = pl.BlockSpec((BLOCK, G * D), lambda g, b: (b, g))
    return pl.pallas_call(
        lambda *refs: block_body(step, *refs),
        grid=(kv, nb),
        in_specs=specs,
        out_specs=[big, big, pl.BlockSpec((G, BLOCK, 2 * D), lambda g, b: (g, b, 0))],
        out_shape=[
            jax.ShapeDtypeStruct((nb * BLOCK, width), f32),
            jax.ShapeDtypeStruct((nb * BLOCK, width), f32),
            jax.ShapeDtypeStruct((kv * G, nb * BLOCK, 2 * D), bf),
        ],
        scratch_shapes=[pltpu.VMEM((2 * BLOCK, 2 * D), bf)] * 3,
        compiler_params=params(10),
        name=f"blocks_{first}_{nb}",
    )(*args)


class Pieces:
    def __init__(self, spans, total):
        self.spans = spans
        self.start = [sum(n for _, n in spans[:i]) for i in range(len(spans))]
        self.first, self.total = spans[0][0], total

    def block(self, j):
        return (j + self.first) % self.total

    def local(self, p):
        s, n = self.start[p], self.spans[p][1]
        return lambda j: jnp.clip(j - s, 0, n - 1)

    def when(self, p, j):
        s, n = self.start[p], self.spans[p][1]
        return pl.when((j >= s) & (j < s + n))


def linear_body(pieces, *refs):
    n = len(pieces.spans)
    fq_refs, part_refs = refs[:n], refs[n : 2 * n]
    before_ref, incl_ref, total_ref, lin_ref, sq_ref, acc = refs[2 * n :]
    j, g = pl.program_id(0), pl.program_id(1)
    ss = lanes(*split((incl_ref[0] - total_ref[0]) + before_ref[...]))
    ss = rows(ss, ss)

    def run(fq_ref, part_ref):
        lin = halves(dot(rows(*[fq_ref[i] for i in range(G)]), ss))
        sq = jnp.zeros((BLOCK, D), f32)
        for i in range(G):
            at = slice(i * D, (i + 1) * D)
            x = lin[i * BLOCK : (i + 1) * BLOCK] + part_ref[:, at]
            lin_ref[:, at] = x
            sq = sq + x * x

        @pl.when(g == 0)
        def _():
            acc[...] = sq

        @pl.when(g > 0)
        def _():
            sq_ref[0] = jnp.sum((acc[...] + sq).T, axis=0, keepdims=True)

    for p in range(n):

        @pieces.when(p, j)
        def _():
            run(fq_refs[p], part_refs[p])


def linear_part(pieces, fq, part, before, incl, total):
    width = part[0].shape[1]
    nb = pieces.total
    kv = total.shape[0]
    assert kv == 2
    fq_specs, part_specs = [], []
    for p in range(len(fq)):
        at = pieces.local(p)
        fq_specs.append(pl.BlockSpec((G, BLOCK, 2 * D), lambda j, g, at=at: (g, at(j), 0)))
        part_specs.append(pl.BlockSpec((BLOCK, G * D), lambda j, g, at=at: (at(j), g)))
    return pl.pallas_call(
        lambda *refs: linear_body(pieces, *refs),
        grid=(nb, kv),
        in_specs=fq_specs
        + part_specs
        + [
            pl.BlockSpec(
                (pl.Squeezed(), pl.Squeezed(), D, D), lambda j, g: (g, pieces.block(j), 0, 0)
            ),
            pl.BlockSpec((1, D, D), lambda j, g: (g, 0, 0)),
            pl.BlockSpec((1, D, D), lambda j, g: (g, 0, 0)),
        ],
        out_specs=[
            pl.BlockSpec((BLOCK, G * D), lambda j, g: (pieces.block(j), g)),
            pl.BlockSpec((1, 1, BLOCK), lambda j, g: (pieces.block(j), 0, 0)),
        ],
        out_shape=[
            jax.ShapeDtypeStruct((nb * BLOCK, width), f32),
            jax.ShapeDtypeStruct((nb, 1, BLOCK), f32),
        ],
        scratch_shapes=[pltpu.VMEM((BLOCK, D), f32)],
        compiler_params=params(12),
        name="linear",
    )(*fq, *part, before, incl, total)


def combine_body(pieces, *refs):
    n = len(pieces.spans)
    win_refs = refs[:n]
    lin_ref, sa_ref, sb_ref, gain_ref, out_ref = refs[n:]
    ms = (sa_ref[0] + sb_ref[0]) * (1.0 / (QUERY_HEADS * D))
    inv = lax.rsqrt(ms + EPS)
    inv = jnp.broadcast_to(inv, (BLOCK, BLOCK)).T
    for p in range(n):

        @pieces.when(p, pl.program_id(0))
        def _():
            for i in range(lin_ref.shape[1] // D):
                at = slice(i * D, (i + 1) * D)
                out_ref[:, at] = lin_ref[:, at] * inv * gain_ref[:, at] + win_refs[p][:, at]


def combine(pieces, win, lin, sa, sb, gain):
    count, width = lin.shape
    nb = count // BLOCK
    big = pl.BlockSpec((BLOCK, width), lambda j, _: (pieces.block(j), 0))
    small = pl.BlockSpec((1, 1, BLOCK), lambda j, _: (pieces.block(j), 0, 0))
    win_specs = []
    for p in range(len(win)):
        at = pieces.local(p)
        win_specs.append(pl.BlockSpec((BLOCK, width), lambda j, _, at=at: (at(j), 0)))
    return pl.pallas_call(
        lambda *refs: combine_body(pieces, *refs),
        grid=(nb, 1),
        in_specs=win_specs
        + [big, small, small, pl.BlockSpec((1, width), lambda j, _: (0, 0))],
        out_specs=big,
        out_shape=jax.ShapeDtypeStruct((count, width), f32),
        compiler_params=params(12),
        name="combine",
    )(*win, lin, sa, sb, gain)


def shards(queries, keys, values, gain):
    count, kv = keys.shape
    nb = count // BLOCK
    peers = lax.axis_size("seq")
    heads = lax.axis_size("head")
    assert heads == 4 and nb == 8 and peers == 32

    tail = jnp.concatenate([keys[count - BLOCK :], values[count - BLOCK :]], axis=1)
    halo = lax.ppermute(tail, "seq", [(i, i + 1) for i in range(peers - 1)])
    before, total = local_states(keys, values)

    def behind(x, by):
        return lax.ppermute(x, "seq", [(i, i + by) for i in range(peers - by)])

    pieces = Pieces([(1, 1), (2, 1), (3, 1), (4, 2), (6, 3)], nb)
    incl = total
    q = pltpu.with_memory_space_constraint(queries, pltpu.HBM)
    done = []
    for number, (first, n) in enumerate(pieces.spans):
        got = behind(incl, 1 << number)
        q, incl = lax.optimization_barrier((q, incl))
        wrap = None
        if first + n > nb:
            wrap = [halo[:, :kv], halo[:, kv:]]
        part = block_part(q, keys, values, first, n, wrap)
        *part, got = lax.optimization_barrier((*part, got))
        done.append(part)
        incl = incl + got
    win, part, fq = zip(*done)
    lin, sq = linear_part(pieces, fq, part, before, incl, total)
    sq = sq + lax.ppermute(sq, "head", [(i, i ^ 1) for i in range(heads)])
    other = lax.ppermute(sq, "head", [(i, i ^ 2) for i in range(heads)])
    return combine(pieces, win, lin, sq, other, gain[None, :])


def solution(mesh):
    in_specs = (P("seq", "head"), P("seq", "head"), P("seq", "head"), P("head"))
    return jax.shard_map(
        shards, mesh=mesh, in_specs=in_specs, out_specs=P("seq", "head"), check_vma=False
    )
```

```python
import math

import jax
import jax.numpy as jnp
from jax import lax
from jax.experimental import pallas as pl
from jax.experimental.pallas import tpu as pltpu
from jax.sharding import PartitionSpec as P

QUERY_HEADS = 64
KEY_VALUE_HEADS = 8
D = 128
G = QUERY_HEADS // KEY_VALUE_HEADS
BLOCK = 128
EPS = 1e-6
SCORE_SCALE = math.log2(math.e) / math.sqrt(D)

f32 = jnp.float32
bf = jnp.bfloat16
NT = (((1,), (1,)), ((), ()))
TN = (((0,), (0,)), ((), ()))


def split(x):
    hi = x.astype(bf)
    return hi, (x - hi.astype(f32)).astype(bf)


def lanes(*xs):
    return jnp.concatenate(xs, axis=1)


def rows(*xs):
    return jnp.concatenate(xs, axis=0)


def dot(a, b, dims=(((1,), (0,)), ((), ()))):
    return lax.dot_general(a, b, dims, preferred_element_type=f32)


def halves(x):
    return x[:, :D] + x[:, D:]


def params(mib):
    return pltpu.CompilerParams(
        vmem_limit_bytes=mib << 20, dimension_semantics=("arbitrary",)
    )


def state_body(k_ref, v_ref, before_ref, pack_ref):
    count = k_ref.shape[0]
    state = jnp.zeros((D, D), f32)
    for b in range(count // BLOCK):
        at = slice(b * BLOCK, (b + 1) * BLOCK)
        before_ref[b] = state
        fh, fl = split(jnp.tanh(k_ref[at, :]))
        vh, vl = split(v_ref[at, :])
        vv = lanes(vh, vl)
        state = state + halves(dot(rows(fh, fl), rows(vv, vv), TN))
    pack_ref[:D] = state
    pack_ref[D : D + BLOCK] = k_ref[count - BLOCK :, :]
    pack_ref[D + BLOCK :] = v_ref[count - BLOCK :, :]


def local_states(keys, values):
    count, width = keys.shape
    kv, nb = width // D, count // BLOCK
    one = pl.Squeezed()
    return pl.pallas_call(
        state_body,
        grid=(kv,),
        in_specs=[pl.BlockSpec((count, D), lambda g: (0, g))] * 2,
        out_specs=[
            pl.BlockSpec((one, nb, D, D), lambda g: (g, 0, 0, 0)),
            pl.BlockSpec((one, D + 2 * BLOCK, D), lambda g: (g, 0, 0)),
        ],
        out_shape=[
            jax.ShapeDtypeStruct((kv, nb, D, D), f32),
            jax.ShapeDtypeStruct((kv, D + 2 * BLOCK, D), f32),
        ],
        compiler_params=params(8),
        name="local_states",
    )(keys, values)


def block_body(wrap, carried, *refs):
    q_ref, k_ref, v_ref, kp_ref, vp_ref, *refs = refs
    if wrap is not None:
        halo_ref, *refs = refs
    win_ref, lin_ref, fq_ref, kh, kl, vv = refs[carried:]
    kv = k_ref.shape[1] // D
    b = pl.program_id(0)
    here = slice(0, BLOCK)
    there = slice(BLOCK, 2 * BLOCK)

    def prepare(g, k, v, at):
        h, l = split(k * SCORE_SCALE)
        kh[g, at, :] = lanes(h, h)
        kl[g, at, :] = lanes(l, l)
        vv[g, at, :] = lanes(*split(v))

    @pl.when(b == 0)
    def _():
        for g in range(kv):
            head = slice(g * D, (g + 1) * D)
            prepare(g, kp_ref[:, head], vp_ref[:, head], there)

    @pl.when(b > 0)
    def _():
        for x in (kh, kl, vv):
            x[:, there, :] = x[:, here, :]

    if wrap is not None:

        @pl.when(b == wrap)
        def _():
            for g in range(kv):
                prepare(g, halo_ref[g, D : D + BLOCK], halo_ref[g, D + BLOCK :], there)

    row = lax.broadcasted_iota(jnp.int32, (BLOCK, BLOCK), 0)
    col = lax.broadcasted_iota(jnp.int32, (BLOCK, BLOCK), 1)
    own = rows(*[row >= col] * G)
    zero = jnp.zeros((BLOCK * G, BLOCK), bf)
    for g in range(kv):
        head = slice(g * D, (g + 1) * D)
        k = k_ref[:, head]
        prepare(g, k, v_ref[:, head], here)
        fh, fl = split(jnp.tanh(k))
        ff = rows(lanes(fh, fh), lanes(fl, fl))
        kk = lanes(kh[g], kl[g])
        v_both = vv[g]
        v_own = vv[g, here, :]
        heads = [slice(i * D, (i + 1) * D) for i in range(g * G, (g + 1) * G)]
        q = rows(*[q_ref[:, at] for at in heads])
        qh, ql = split(q)
        s = dot(lanes(qh, ql, qh, ql), kk, NT)
        f2 = lanes(*split(jnp.tanh(q)))
        fq_ref[0, g * G * BLOCK : (g + 1) * G * BLOCK, :] = f2
        a = jnp.where(own, halves(dot(f2, ff, NT)), 0.0)
        lin = halves(dot(lanes(*split(a)), rows(v_own, v_own)))
        before = s[:, BLOCK:]
        if wrap is not None:
            before = jnp.where((lax.axis_index("seq") > 0) | (b != wrap), before, -1e30)
        t = jnp.where(own, s[:, :BLOCK], before)
        p = jnp.exp2(t - jnp.max(t, axis=1, keepdims=True))
        total = jnp.sum(p, axis=1, keepdims=True)
        ph, pl_ = split(p)
        p4 = lanes(
            jnp.where(own, ph, zero),
            jnp.where(own, zero, ph),
            jnp.where(own, pl_, zero),
            jnp.where(own, zero, pl_),
        )
        win = halves(dot(p4, rows(v_both, v_both))) * (1.0 / total)
        for i, at in enumerate(heads):
            win_ref[:, at] = win[i * BLOCK : (i + 1) * BLOCK]
            lin_ref[:, at] = lin[i * BLOCK : (i + 1) * BLOCK]


def block_part(queries, keys, values, first, n, made, halo=None):
    count, width = queries.shape
    kv = keys.shape[1] // D
    nb = count // BLOCK
    own = lambda b: ((first + b) % nb, 0)
    prior = lambda b: (first - 1, 0)
    small = lambda index: pl.BlockSpec((BLOCK, kv * D), index)
    args = [queries, keys, values, keys, values]
    specs = [pl.BlockSpec((BLOCK, width), own), small(own), small(own), small(prior), small(prior)]
    wrap = None
    if halo is not None:
        wrap = nb - first
        args.append(halo)
        specs.append(pl.BlockSpec(halo.shape, lambda b: (0, 0, 0)))
    aliases = {len(args) + i: i for i in range(len(made))}
    big = pl.BlockSpec((BLOCK, width), own)
    return pl.pallas_call(
        lambda *refs: block_body(wrap, len(made), *refs),
        grid=(n,),
        in_specs=specs + [pl.BlockSpec(memory_space=pl.ANY)] * len(made),
        out_specs=[
            big,
            big,
            pl.BlockSpec((1, kv * G * BLOCK, 2 * D), lambda b: ((first + b) % nb, 0, 0)),
        ],
        out_shape=[
            pltpu.VMEM((count, width), f32),
            pltpu.VMEM((count, width), f32),
            pltpu.VMEM((nb, kv * G * BLOCK, 2 * D), bf),
        ],
        scratch_shapes=[pltpu.VMEM((kv, 2 * BLOCK, 2 * D), bf)] * 3,
        input_output_aliases=aliases,
        compiler_params=params(12),
        name=f"blocks_{first}_{n}",
    )(*args, *made)


def linear_body(fq_ref, part_ref, before_ref, incl_ref, pack_ref, lin_ref, sq_ref):
    sq = jnp.zeros((BLOCK, D), f32)
    for g in range(incl_ref.shape[0]):
        ss = lanes(*split((incl_ref[g] - pack_ref[g]) + before_ref[g, 0]))
        fq = fq_ref[0, g * G * BLOCK : (g + 1) * G * BLOCK, :]
        lin = halves(dot(fq, rows(ss, ss)))
        for i in range(G):
            at = slice((g * G + i) * D, (g * G + i + 1) * D)
            x = lin[i * BLOCK : (i + 1) * BLOCK] + part_ref[:, at]
            lin_ref[:, at] = x
            sq = sq + x * x
    sq_ref[0] = jnp.sum(sq.T, axis=0, keepdims=True)


def linear_part(fq, part, before, incl, pack):
    count, width = part.shape
    kv, nb = before.shape[:2]
    big = pl.BlockSpec((BLOCK, width), lambda b: (b, 0))
    return pl.pallas_call(
        linear_body,
        grid=(nb,),
        in_specs=[
            pl.BlockSpec((1,) + fq.shape[1:], lambda b: (b, 0, 0)),
            big,
            pl.BlockSpec((kv, 1, D, D), lambda b: (0, b, 0, 0)),
            pl.BlockSpec((kv, D, D), lambda b: (0, 0, 0)),
            pl.BlockSpec((kv, D, D), lambda b: (0, 0, 0)),
        ],
        out_specs=[big, pl.BlockSpec((1, 1, BLOCK), lambda b: (b, 0, 0))],
        out_shape=[
            pltpu.VMEM((count, width), f32),
            pltpu.VMEM((nb, 1, BLOCK), f32),
        ],
        compiler_params=params(8),
        name="linear",
    )(fq, part, before, incl, pack)


def combine_body(lin_ref, win_ref, sa_ref, sb_ref, gain_ref, out_ref):
    for r in range(lin_ref.shape[0] // BLOCK):
        ms = (sa_ref[r] + sb_ref[r]) * (1.0 / (QUERY_HEADS * D))
        inv = jnp.broadcast_to(lax.rsqrt(ms + EPS), (BLOCK, BLOCK)).T
        row = slice(r * BLOCK, (r + 1) * BLOCK)
        for i in range(lin_ref.shape[1] // D):
            at = slice(i * D, (i + 1) * D)
            out_ref[row, at] = lin_ref[row, at] * inv * gain_ref[:, at] + win_ref[row, at]


def combine(lin, win, sa, sb, gain):
    count, width = lin.shape
    n = 2
    big = pl.BlockSpec((n * BLOCK, width), lambda j: (j, 0))
    small = pl.BlockSpec((n, 1, BLOCK), lambda j: (j, 0, 0))
    return pl.pallas_call(
        combine_body,
        grid=(count // (n * BLOCK),),
        in_specs=[big, big, small, small, pl.BlockSpec((1, width), lambda j: (0, 0))],
        out_specs=big,
        out_shape=jax.ShapeDtypeStruct((count, width), f32),
        compiler_params=params(8),
        name="combine",
    )(lin, win, sa, sb, gain)


def shards(queries, keys, values, gain):
    count = queries.shape[0]
    nb = count // BLOCK
    peers = lax.axis_size("seq")
    heads = lax.axis_size("head")
    assert heads == 4 and nb == 8 and peers == 32
    queries, keys, values = (
        pltpu.with_memory_space_constraint(x, pltpu.HBM) for x in (queries, keys, values)
    )

    def behind(x, by):
        return lax.ppermute(x, "seq", [(i, i + by) for i in range(peers - by)])

    before, pack = local_states(keys, values)
    incl = pack
    made = []
    halo = None
    for number, (first, n) in enumerate([(1, 2), (3, 1), (4, 1), (5, 1), (6, 3)]):
        got = behind(incl, 1 << number)
        if made:
            *made, incl = lax.optimization_barrier((*made, incl))
        made = block_part(
            queries, keys, values, first, n, made, halo if first + n > nb else None
        )
        *made, got = lax.optimization_barrier((*made, got))
        if number == 0:
            halo = got
        incl = incl[:, :D] + got[:, :D]
    win, part, fq = made
    lin, sq = linear_part(fq, part, before, incl, pack)
    sq = sq + lax.ppermute(sq, "head", [(i, i ^ 1) for i in range(heads)])
    other = lax.ppermute(sq, "head", [(i, i ^ 2) for i in range(heads)])
    return combine(lin, win, sq, other, gain[None, :])


def solution(mesh):
    in_specs = (P("seq", "head"), P("seq", "head"), P("seq", "head"), P("head"))
    return jax.shard_map(
        shards, mesh=mesh, in_specs=in_specs, out_specs=P("seq", "head"), check_vma=False
    )
```

```python
import math

import jax
import jax.numpy as jnp
from jax import lax
from jax.experimental import pallas as pl
from jax.experimental.pallas import tpu as pltpu
from jax.sharding import PartitionSpec as P

QUERY_HEADS = 64
KEY_VALUE_HEADS = 8
D = 128
G = QUERY_HEADS // KEY_VALUE_HEADS
BLOCK = 128
EPS = 1e-6
SCORE_SCALE = math.log2(math.e) / math.sqrt(D)

f32 = jnp.float32
bf = jnp.bfloat16
NT = (((1,), (1,)), ((), ()))
TN = (((0,), (0,)), ((), ()))


def split(x):
    hi = x.astype(bf)
    return hi, (x - hi.astype(f32)).astype(bf)


def lanes(*xs):
    return jnp.concatenate(xs, axis=1)


def rows(*xs):
    return jnp.concatenate(xs, axis=0)


def dot(a, b, dims=(((1,), (0,)), ((), ()))):
    return lax.dot_general(a, b, dims, preferred_element_type=f32)


def halves(x):
    return x[:, :D] + x[:, D:]


def params(mib):
    return pltpu.CompilerParams(
        vmem_limit_bytes=mib << 20, dimension_semantics=("arbitrary",)
    )


def state_body(k_ref, v_ref, before_ref, total_ref, tail_ref):
    count = k_ref.shape[0]
    state = jnp.zeros((D, D), f32)
    for b in range(count // BLOCK):
        at = slice(b * BLOCK, (b + 1) * BLOCK)
        before_ref[b] = state
        fh, fl = split(jnp.tanh(k_ref[at, :]))
        vh, vl = split(v_ref[at, :])
        vv = lanes(vh, vl)
        state = state + halves(dot(rows(fh, fl), rows(vv, vv), TN))
    total_ref[...] = state
    tail_ref[:BLOCK] = k_ref[count - BLOCK :, :]
    tail_ref[BLOCK:] = v_ref[count - BLOCK :, :]


def local_states(keys, values):
    count, width = keys.shape
    kv, nb = width // D, count // BLOCK
    one = pl.Squeezed()
    return pl.pallas_call(
        state_body,
        grid=(kv,),
        in_specs=[pl.BlockSpec((count, D), lambda g: (0, g))] * 2,
        out_specs=[
            pl.BlockSpec((one, nb, D, D), lambda g: (g, 0, 0, 0)),
            pl.BlockSpec((one, D, D), lambda g: (g, 0, 0)),
            pl.BlockSpec((one, 2 * BLOCK, D), lambda g: (g, 0, 0)),
        ],
        out_shape=[
            jax.ShapeDtypeStruct((kv, nb, D, D), f32),
            jax.ShapeDtypeStruct((kv, D, D), f32),
            jax.ShapeDtypeStruct((kv, 2 * BLOCK, D), f32),
        ],
        compiler_params=params(8),
        name="local_states",
    )(keys, values)


def place():
    i = lax.axis_index("seq")
    return i // 8, (i // 2) % 4, i % 2


def chip_body(own_ref, other_ref, out_ref):
    core = place()[2]
    out_ref[...] = own_ref[core] + other_ref[core]


def row_body(own_ref, one_ref, two_ref, three_ref, sum_ref, before_ref):
    x = place()[1]
    got = [one_ref[...], two_ref[...], three_ref[...]]
    sum_ref[...] = own_ref[...] + got[0] + got[1] + got[2]
    before = jnp.zeros((D, D), f32)
    for by, state in enumerate(got, 1):
        before = before + jnp.where(x >= by, state, 0.0)
    before_ref[...] = before


def small_call(body, outs, name, *args):
    shape = jax.ShapeDtypeStruct((D, D), f32)
    return pl.pallas_call(
        body,
        out_shape=[shape] * outs,
        compiler_params=pltpu.CompilerParams(vmem_limit_bytes=2 << 20),
        name=name,
    )(*args)


def block_body(wrap, carried, *refs):
    q_ref, k_ref, v_ref, kp_ref, vp_ref, *refs = refs
    if wrap is not None:
        halo_ref, *refs = refs
    win_ref, lin_ref, fq_ref, kh, kl, vv = refs[carried:]
    kv = k_ref.shape[1] // D
    b = pl.program_id(0)
    here = slice(0, BLOCK)
    there = slice(BLOCK, 2 * BLOCK)

    def prepare(g, k, v, at):
        h, l = split(k * SCORE_SCALE)
        kh[g, at, :] = lanes(h, h)
        kl[g, at, :] = lanes(l, l)
        vv[g, at, :] = lanes(*split(v))

    @pl.when(b == 0)
    def _():
        for g in range(kv):
            head = slice(g * D, (g + 1) * D)
            prepare(g, kp_ref[:, head], vp_ref[:, head], there)

    @pl.when(b > 0)
    def _():
        for x in (kh, kl, vv):
            x[:, there, :] = x[:, here, :]

    if wrap is not None:

        @pl.when(b == wrap)
        def _():
            for g in range(kv):
                prepare(g, halo_ref[g, :BLOCK], halo_ref[g, BLOCK:], there)

    row = lax.broadcasted_iota(jnp.int32, (BLOCK, BLOCK), 0)
    col = lax.broadcasted_iota(jnp.int32, (BLOCK, BLOCK), 1)
    own = rows(*[row >= col] * G)
    zero = jnp.zeros((BLOCK * G, BLOCK), bf)
    for g in range(kv):
        head = slice(g * D, (g + 1) * D)
        k = k_ref[:, head]
        prepare(g, k, v_ref[:, head], here)
        fh, fl = split(jnp.tanh(k))
        ff = rows(lanes(fh, fh), lanes(fl, fl))
        kk = lanes(kh[g], kl[g])
        v_both = vv[g]
        v_own = vv[g, here, :]
        heads = [slice(i * D, (i + 1) * D) for i in range(g * G, (g + 1) * G)]
        q = rows(*[q_ref[:, at] for at in heads])
        qh, ql = split(q)
        s = dot(lanes(qh, ql, qh, ql), kk, NT)
        f2 = lanes(*split(jnp.tanh(q)))
        fq_ref[0, g * G * BLOCK : (g + 1) * G * BLOCK, :] = f2
        a = jnp.where(own, halves(dot(f2, ff, NT)), 0.0)
        lin = halves(dot(lanes(*split(a)), rows(v_own, v_own)))
        before = s[:, BLOCK:]
        if wrap is not None:
            before = jnp.where((lax.axis_index("seq") > 0) | (b != wrap), before, -1e30)
        t = jnp.where(own, s[:, :BLOCK], before)
        p = jnp.exp2(t - jnp.max(t, axis=1, keepdims=True))
        total = jnp.sum(p, axis=1, keepdims=True)
        ph, pl_ = split(p)
        p4 = lanes(
            jnp.where(own, ph, zero),
            jnp.where(own, zero, ph),
            jnp.where(own, pl_, zero),
            jnp.where(own, zero, pl_),
        )
        win = halves(dot(p4, rows(v_both, v_both))) * (1.0 / total)
        for i, at in enumerate(heads):
            win_ref[:, at] = win[i * BLOCK : (i + 1) * BLOCK]
            lin_ref[:, at] = lin[i * BLOCK : (i + 1) * BLOCK]


def block_part(queries, keys, values, first, n, made, halo=None):
    count, width = queries.shape
    kv = keys.shape[1] // D
    nb = count // BLOCK
    own = lambda b: ((first + b) % nb, 0)
    prior = lambda b: (first - 1, 0)
    small = lambda index: pl.BlockSpec((BLOCK, kv * D), index)
    args = [queries, keys, values, keys, values]
    specs = [pl.BlockSpec((BLOCK, width), own), small(own), small(own), small(prior), small(prior)]
    wrap = None
    if halo is not None:
        wrap = nb - first
        args.append(halo)
        specs.append(pl.BlockSpec(halo.shape, lambda b: (0, 0, 0)))
    aliases = {len(args) + i: i for i in range(len(made))}
    big = pl.BlockSpec((BLOCK, width), own)
    return pl.pallas_call(
        lambda *refs: block_body(wrap, len(made), *refs),
        grid=(n,),
        in_specs=specs + [pl.BlockSpec(memory_space=pl.ANY)] * len(made),
        out_specs=[
            big,
            big,
            pl.BlockSpec((1, kv * G * BLOCK, 2 * D), lambda b: ((first + b) % nb, 0, 0)),
        ],
        out_shape=[
            pltpu.VMEM((count, width), f32),
            pltpu.VMEM((count, width), f32),
            pltpu.VMEM((nb, kv * G * BLOCK, 2 * D), bf),
        ],
        scratch_shapes=[pltpu.VMEM((kv, 2 * BLOCK, 2 * D), bf)] * 3,
        input_output_aliases=aliases,
        compiler_params=params(12),
        name=f"blocks_{first}_{n}",
    )(*args, *made)


def linear_body(fq_ref, part_ref, inner_ref, mine_ref, their_ref, other_ref, lin_ref, sq_ref):
    core = place()[2]
    sq = jnp.zeros((BLOCK, D), f32)
    for g in range(other_ref.shape[0]):
        state = jnp.where(core == g, mine_ref[...], their_ref[...])
        state = state + jnp.where(core == 1, other_ref[g], 0.0) + inner_ref[g, 0]
        ss = lanes(*split(state))
        fq = fq_ref[0, g * G * BLOCK : (g + 1) * G * BLOCK, :]
        lin = halves(dot(fq, rows(ss, ss)))
        for i in range(G):
            at = slice((g * G + i) * D, (g * G + i + 1) * D)
            x = lin[i * BLOCK : (i + 1) * BLOCK] + part_ref[:, at]
            lin_ref[:, at] = x
            sq = sq + x * x
    sq_ref[0] = jnp.sum(sq.T, axis=0, keepdims=True)


def linear_part(fq, part, inner, mine, theirs, other):
    count, width = part.shape
    kv, nb = inner.shape[:2]
    big = pl.BlockSpec((BLOCK, width), lambda b: (b, 0))
    state = pl.BlockSpec((D, D), lambda b: (0, 0))
    return pl.pallas_call(
        linear_body,
        grid=(nb,),
        in_specs=[
            pl.BlockSpec((1,) + fq.shape[1:], lambda b: (b, 0, 0)),
            big,
            pl.BlockSpec((kv, 1, D, D), lambda b: (0, b, 0, 0)),
            state,
            state,
            pl.BlockSpec((kv, D, D), lambda b: (0, 0, 0)),
        ],
        out_specs=[big, pl.BlockSpec((1, 1, BLOCK), lambda b: (b, 0, 0))],
        out_shape=[
            pltpu.VMEM((count, width), f32),
            pltpu.VMEM((nb, 1, BLOCK), f32),
        ],
        compiler_params=params(8),
        name="linear",
    )(fq, part, inner, mine, theirs, other)


def combine_body(lin_ref, win_ref, sa_ref, sb_ref, gain_ref, out_ref):
    for r in range(lin_ref.shape[0] // BLOCK):
        ms = (sa_ref[r] + sb_ref[r]) * (1.0 / (QUERY_HEADS * D))
        inv = jnp.broadcast_to(lax.rsqrt(ms + EPS), (BLOCK, BLOCK)).T
        row = slice(r * BLOCK, (r + 1) * BLOCK)
        for i in range(lin_ref.shape[1] // D):
            at = slice(i * D, (i + 1) * D)
            out_ref[row, at] = lin_ref[row, at] * inv * gain_ref[:, at] + win_ref[row, at]


def combine(lin, win, sa, sb, gain):
    count, width = lin.shape
    n = 2
    big = pl.BlockSpec((n * BLOCK, width), lambda j: (j, 0))
    small = pl.BlockSpec((n, 1, BLOCK), lambda j: (j, 0, 0))
    return pl.pallas_call(
        combine_body,
        grid=(count // (n * BLOCK),),
        in_specs=[big, big, small, small, pl.BlockSpec((1, width), lambda j: (0, 0))],
        out_specs=big,
        out_shape=jax.ShapeDtypeStruct((count, width), f32),
        compiler_params=params(8),
        name="combine",
    )(lin, win, sa, sb, gain)


def chips(dy, dx, wrap):
    pairs = []
    for i in range(32):
        y, x, core = i // 8 + dy, (i // 2) % 4 + dx, i % 2
        if wrap or (y < 4 and x < 4):
            pairs.append((i, (y % 4) * 8 + (x % 4) * 2 + core))
    return pairs


SWAP = [(i, i ^ 1) for i in range(32)]


def shards(queries, keys, values, gain):
    count = queries.shape[0]
    nb = count // BLOCK
    heads = lax.axis_size("head")
    assert heads == 4 and nb == 8 and lax.axis_size("seq") == 32
    queries, keys, values = (
        pltpu.with_memory_space_constraint(x, pltpu.HBM) for x in (queries, keys, values)
    )

    def move(x, pairs):
        return lax.ppermute(x, "seq", pairs)

    def tie(*xs):
        return lax.optimization_barrier(xs)

    inner, total, tail = local_states(keys, values)
    other = move(total, SWAP)
    (chip,) = small_call(chip_body, 1, "chip_sum", total, other)
    along_x = [move(chip, chips(0, by, True)) for by in (1, 2, 3)]
    halo = move(tail, [(i, i + 1) for i in range(31)])
    tail, chip = tie(tail, chip)
    made = block_part(queries, keys, values, 1, 3, ())
    *made, one, two, three = tie(*made, *along_x)
    row, before = small_call(row_body, 2, "row_sum", chip, one, two, three)
    along_y = [move(row, chips(by, 0, False)) for by in (1, 2, 3)]
    *made, before = tie(*made, before)
    made = block_part(queries, keys, values, 4, 2, made)
    *made, one, two, three = tie(*made, *along_y)
    mine = before + one + two + three
    theirs = move(mine, SWAP)
    *made, mine = tie(*made, mine)
    win, part, fq = block_part(queries, keys, values, 6, 3, made, halo)
    lin, sq = linear_part(fq, part, inner, mine, theirs, other)
    sq = sq + lax.ppermute(sq, "head", [(i, i ^ 1) for i in range(heads)])
    across = lax.ppermute(sq, "head", [(i, i ^ 2) for i in range(heads)])
    return combine(lin, win, sq, across, gain[None, :])


def solution(mesh):
    in_specs = (P("seq", "head"), P("seq", "head"), P("seq", "head"), P("head"))
    return jax.shard_map(
        shards, mesh=mesh, in_specs=in_specs, out_specs=P("seq", "head"), check_vma=False
    )
```

```python
import math

import jax
import jax.numpy as jnp
from jax import lax
from jax.experimental import pallas as pl
from jax.experimental.pallas import tpu as pltpu
from jax.sharding import PartitionSpec as P

QUERY_HEADS = 64
KEY_VALUE_HEADS = 8
D = 128
G = QUERY_HEADS // KEY_VALUE_HEADS
BLOCK = 128
EPS = 1e-6
SCORE_SCALE = math.log2(math.e) / math.sqrt(D)

f32 = jnp.float32
bf = jnp.bfloat16
NT = (((1,), (1,)), ((), ()))
TN = (((0,), (0,)), ((), ()))


def split(x):
    hi = x.astype(bf)
    return hi, (x - hi.astype(f32)).astype(bf)


def lanes(*xs):
    return jnp.concatenate(xs, axis=1)


def rows(*xs):
    return jnp.concatenate(xs, axis=0)


def dot(a, b, dims=(((1,), (0,)), ((), ()))):
    return lax.dot_general(a, b, dims, preferred_element_type=f32)


def halves(x):
    return x[:, :D] + x[:, D:]


def params(mib):
    return pltpu.CompilerParams(
        vmem_limit_bytes=mib << 20, dimension_semantics=("arbitrary",)
    )


def state_body(k_ref, v_ref, before_ref, total_ref, tail_ref):
    count = k_ref.shape[0]
    state = jnp.zeros((D, D), f32)
    for b in range(count // BLOCK):
        at = slice(b * BLOCK, (b + 1) * BLOCK)
        before_ref[b] = state
        fh, fl = split(jnp.tanh(k_ref[at, :]))
        vh, vl = split(v_ref[at, :])
        vv = lanes(vh, vl)
        state = state + halves(dot(rows(fh, fl), rows(vv, vv), TN))
    total_ref[...] = state
    tail_ref[:BLOCK] = k_ref[count - BLOCK :, :]
    tail_ref[BLOCK:] = v_ref[count - BLOCK :, :]


def local_states(keys, values):
    count, width = keys.shape
    kv, nb = width // D, count // BLOCK
    one = pl.Squeezed()
    return pl.pallas_call(
        state_body,
        grid=(kv,),
        in_specs=[pl.BlockSpec((count, D), lambda g: (0, g))] * 2,
        out_specs=[
            pl.BlockSpec((one, nb, D, D), lambda g: (g, 0, 0, 0)),
            pl.BlockSpec((one, D, D), lambda g: (g, 0, 0)),
            pl.BlockSpec((one, 2 * BLOCK, D), lambda g: (g, 0, 0)),
        ],
        out_shape=[
            jax.ShapeDtypeStruct((kv, nb, D, D), f32),
            jax.ShapeDtypeStruct((kv, D, D), f32),
            jax.ShapeDtypeStruct((kv, 2 * BLOCK, D), f32),
        ],
        compiler_params=params(8),
        name="local_states",
    )(keys, values)


def place():
    i = lax.axis_index("seq")
    return i // 8, (i // 2) % 4, i % 2


def chip_body(own_ref, other_ref, out_ref):
    core = place()[2]
    out_ref[...] = own_ref[core] + other_ref[core]


def row_body(own_ref, one_ref, two_ref, three_ref, sum_ref, before_ref):
    x = place()[1]
    got = [one_ref[...], two_ref[...], three_ref[...]]
    sum_ref[...] = own_ref[...] + got[0] + got[1] + got[2]
    before = jnp.zeros((D, D), f32)
    for by, state in enumerate(got, 1):
        before = before + jnp.where(x >= by, state, 0.0)
    before_ref[...] = before


def small_call(body, outs, name, *args):
    shape = jax.ShapeDtypeStruct((D, D), f32)
    return pl.pallas_call(
        body,
        out_shape=[shape] * outs,
        compiler_params=pltpu.CompilerParams(vmem_limit_bytes=2 << 20),
        name=name,
    )(*args)


def block_body(wrap, carried, *refs):
    q_ref, k_ref, v_ref, kp_ref, vp_ref, *refs = refs
    if wrap is not None:
        halo_ref, *refs = refs
    win_ref, lin_ref, fq_ref, kh, kl, vv = refs[carried:]
    kv = k_ref.shape[1] // D
    b = pl.program_id(0)
    here = slice(0, BLOCK)
    there = slice(BLOCK, 2 * BLOCK)

    def prepare(g, k, v, at):
        h, l = split(k * SCORE_SCALE)
        kh[g, at, :] = lanes(h, h)
        kl[g, at, :] = lanes(l, l)
        vv[g, at, :] = lanes(*split(v))

    @pl.when(b == 0)
    def _():
        for g in range(kv):
            head = slice(g * D, (g + 1) * D)
            prepare(g, kp_ref[:, head], vp_ref[:, head], there)

    @pl.when(b > 0)
    def _():
        for x in (kh, kl, vv):
            x[:, there, :] = x[:, here, :]

    if wrap is not None:

        @pl.when(b == wrap)
        def _():
            for g in range(kv):
                prepare(g, halo_ref[g, :BLOCK], halo_ref[g, BLOCK:], there)

    row = lax.broadcasted_iota(jnp.int32, (BLOCK, BLOCK), 0)
    col = lax.broadcasted_iota(jnp.int32, (BLOCK, BLOCK), 1)
    own = rows(*[row >= col] * G)
    zero = jnp.zeros((BLOCK * G, BLOCK), bf)
    for g in range(kv):
        head = slice(g * D, (g + 1) * D)
        k = k_ref[:, head]
        prepare(g, k, v_ref[:, head], here)
        fh, fl = split(jnp.tanh(k))
        ff = rows(lanes(fh, fh), lanes(fl, fl))
        kk = lanes(kh[g], kl[g])
        v_both = vv[g]
        v_own = vv[g, here, :]
        heads = [slice(i * D, (i + 1) * D) for i in range(g * G, (g + 1) * G)]
        q = rows(*[q_ref[:, at] for at in heads])
        qh, ql = split(q)
        s = dot(lanes(qh, ql, qh, ql), kk, NT)
        f2 = lanes(*split(jnp.tanh(q)))
        fq_ref[0, g * G * BLOCK : (g + 1) * G * BLOCK, :] = f2
        a = jnp.where(own, halves(dot(f2, ff, NT)), 0.0)
        lin = halves(dot(lanes(*split(a)), rows(v_own, v_own)))
        before = s[:, BLOCK:]
        if wrap is not None:
            before = jnp.where((lax.axis_index("seq") > 0) | (b != wrap), before, -1e30)
        t = jnp.where(own, s[:, :BLOCK], before)
        p = jnp.exp2(t - jnp.max(t, axis=1, keepdims=True))
        total = jnp.sum(p, axis=1, keepdims=True)
        ph, pl_ = split(p)
        p4 = lanes(
            jnp.where(own, ph, zero),
            jnp.where(own, zero, ph),
            jnp.where(own, pl_, zero),
            jnp.where(own, zero, pl_),
        )
        win = halves(dot(p4, rows(v_both, v_both))) * (1.0 / total)
        for i, at in enumerate(heads):
            win_ref[:, at] = win[i * BLOCK : (i + 1) * BLOCK]
            lin_ref[:, at] = lin[i * BLOCK : (i + 1) * BLOCK]


def block_part(queries, keys, values, first, n, made, halo=None):
    count, width = queries.shape
    kv = keys.shape[1] // D
    nb = count // BLOCK
    own = lambda b: ((first + b) % nb, 0)
    prior = lambda b: (first - 1, 0)
    small = lambda index: pl.BlockSpec((BLOCK, kv * D), index)
    args = [queries, keys, values, keys, values]
    specs = [pl.BlockSpec((BLOCK, width), own), small(own), small(own), small(prior), small(prior)]
    wrap = None
    if halo is not None:
        wrap = nb - first
        args.append(halo)
        specs.append(pl.BlockSpec(halo.shape, lambda b: (0, 0, 0)))
    aliases = {len(args) + i: i for i in range(len(made))}
    big = pl.BlockSpec((BLOCK, width), own)
    return pl.pallas_call(
        lambda *refs: block_body(wrap, len(made), *refs),
        grid=(n,),
        in_specs=specs + [pl.BlockSpec(memory_space=pl.ANY)] * len(made),
        out_specs=[
            big,
            big,
            pl.BlockSpec((1, kv * G * BLOCK, 2 * D), lambda b: ((first + b) % nb, 0, 0)),
        ],
        out_shape=[
            pltpu.VMEM((count, width), f32),
            pltpu.VMEM((count, width), f32),
            pltpu.VMEM((nb, kv * G * BLOCK, 2 * D), bf),
        ],
        scratch_shapes=[pltpu.VMEM((kv, 2 * BLOCK, 2 * D), bf)] * 3,
        input_output_aliases=aliases,
        compiler_params=params(12),
        name=f"blocks_{first}_{n}",
    )(*args, *made)


def linear_body(fq_ref, part_ref, inner_ref, mine_ref, their_ref, other_ref, lin_ref, sq_ref):
    core = place()[2]
    sq = jnp.zeros((BLOCK, D), f32)
    for g in range(other_ref.shape[0]):
        state = jnp.where(core == g, mine_ref[...], their_ref[...])
        state = state + jnp.where(core == 1, other_ref[g], 0.0) + inner_ref[g, 0]
        ss = lanes(*split(state))
        fq = fq_ref[0, g * G * BLOCK : (g + 1) * G * BLOCK, :]
        lin = halves(dot(fq, rows(ss, ss)))
        for i in range(G):
            at = slice((g * G + i) * D, (g * G + i + 1) * D)
            x = lin[i * BLOCK : (i + 1) * BLOCK] + part_ref[:, at]
            lin_ref[:, at] = x
            sq = sq + x * x
    sq_ref[0] = jnp.sum(sq.T, axis=0, keepdims=True)


def linear_part(fq, part, inner, mine, theirs, other):
    count, width = part.shape
    kv, nb = inner.shape[:2]
    big = pl.BlockSpec((BLOCK, width), lambda b: (b, 0))
    state = pl.BlockSpec((D, D), lambda b: (0, 0))
    return pl.pallas_call(
        linear_body,
        grid=(nb,),
        in_specs=[
            pl.BlockSpec((1,) + fq.shape[1:], lambda b: (b, 0, 0)),
            big,
            pl.BlockSpec((kv, 1, D, D), lambda b: (0, b, 0, 0)),
            state,
            state,
            pl.BlockSpec((kv, D, D), lambda b: (0, 0, 0)),
        ],
        out_specs=[big, pl.BlockSpec((1, 1, BLOCK), lambda b: (b, 0, 0))],
        out_shape=[
            pltpu.VMEM((count, width), f32),
            pltpu.VMEM((nb, 1, BLOCK), f32),
        ],
        compiler_params=params(8),
        name="linear",
    )(fq, part, inner, mine, theirs, other)


def combine_body(lin_ref, win_ref, sa_ref, sb_ref, gain_ref, out_ref):
    for r in range(lin_ref.shape[0] // BLOCK):
        ms = (sa_ref[r] + sb_ref[r]) * (1.0 / (QUERY_HEADS * D))
        inv = jnp.broadcast_to(lax.rsqrt(ms + EPS), (BLOCK, BLOCK)).T
        row = slice(r * BLOCK, (r + 1) * BLOCK)
        for i in range(lin_ref.shape[1] // D):
            at = slice(i * D, (i + 1) * D)
            out_ref[row, at] = lin_ref[row, at] * inv * gain_ref[:, at] + win_ref[row, at]


def combine(lin, win, sa, sb, gain):
    count, width = lin.shape
    n = 2
    big = pl.BlockSpec((n * BLOCK, width), lambda j: (j, 0))
    small = pl.BlockSpec((n, 1, BLOCK), lambda j: (j, 0, 0))
    return pl.pallas_call(
        combine_body,
        grid=(count // (n * BLOCK),),
        in_specs=[big, big, small, small, pl.BlockSpec((1, width), lambda j: (0, 0))],
        out_specs=big,
        out_shape=jax.ShapeDtypeStruct((count, width), f32),
        compiler_params=params(8),
        name="combine",
    )(lin, win, sa, sb, gain)


def shift_x(by):
    return [(i, i // 8 * 8 + (i + 2 * by) % 8) for i in range(32)]


def down_from(y):
    return [(y * 8 + i, (y + 1) * 8 + i) for i in range(8)]


SWAP = [(i, i ^ 1) for i in range(32)]


def shards(queries, keys, values, gain):
    count = queries.shape[0]
    nb = count // BLOCK
    heads = lax.axis_size("head")
    assert heads == 4 and nb == 8 and lax.axis_size("seq") == 32
    queries, keys, values = (
        pltpu.with_memory_space_constraint(x, pltpu.HBM) for x in (queries, keys, values)
    )

    def move(x, pairs):
        return lax.ppermute(x, "seq", pairs)

    def tie(*xs):
        return lax.optimization_barrier(xs)

    inner, total, tail = local_states(keys, values)
    other = move(total, SWAP)
    (chip,) = small_call(chip_body, 1, "chip_sum", total, other)
    along_x = [move(chip, shift_x(by)) for by in (1, 2, 3)]
    halo = move(tail, [(i, i + 1) for i in range(31)])
    made = block_part(queries, keys, values, 1, 2, ())
    *made, one, two, three = tie(*made, *along_x)
    row, mine = small_call(row_body, 2, "row_sum", chip, one, two, three)
    for y, first in enumerate((3, 5, 7)):
        got = move(row, down_from(y))
        *made, mine = tie(*made, mine)
        made = block_part(queries, keys, values, first, 2, made, halo if first == 7 else None)
        *made, got = tie(*made, got)
        row, mine = row + got, mine + got
    theirs = move(mine, SWAP)
    win, part, fq = made
    lin, sq = linear_part(fq, part, inner, mine, theirs, other)
    sq = sq + lax.ppermute(sq, "head", [(i, i ^ 1) for i in range(heads)])
    across = lax.ppermute(sq, "head", [(i, i ^ 2) for i in range(heads)])
    return combine(lin, win, sq, across, gain[None, :])


def solution(mesh):
    in_specs = (P("seq", "head"), P("seq", "head"), P("seq", "head"), P("head"))
    return jax.shard_map(
        shards, mesh=mesh, in_specs=in_specs, out_specs=P("seq", "head"), check_vma=False
    )
```

```python
import functools
import math

import jax
import jax.numpy as jnp
from jax import lax
from jax.experimental import pallas as pl
from jax.experimental.pallas import tpu as pltpu
from jax.sharding import PartitionSpec as P

QUERY_HEADS = 64
KEY_VALUE_HEADS = 8
D = 128
G = QUERY_HEADS // KEY_VALUE_HEADS
BLOCK = 128
STEP = 2
EPS = 1e-6
SCORE_SCALE = math.log2(math.e) / math.sqrt(D)

f32 = jnp.float32
bf = jnp.bfloat16
NT = (((1,), (1,)), ((), ()))
TN = (((0,), (0,)), ((), ()))


def split(x):
    hi = x.astype(bf)
    return hi, (x - hi.astype(f32)).astype(bf)


def lanes(*xs):
    return jnp.concatenate(xs, axis=1)


def rows(*xs):
    return jnp.concatenate(xs, axis=0)


def dot(a, b, dims=(((1,), (0,)), ((), ()))):
    return lax.dot_general(a, b, dims, preferred_element_type=f32)


def halves(x):
    return x[:, :D] + x[:, D:]


def params(mib):
    return pltpu.CompilerParams(
        vmem_limit_bytes=mib << 20, dimension_semantics=("arbitrary",)
    )


def state_body(
    k_ref, v_ref, q_hbm, before_ref, total_ref, tail_ref, kp_ref, vp_ref, q_ref, sem, *, ahead
):
    count = k_ref.shape[0]
    g = pl.program_id(0)
    fetch = pltpu.make_async_copy(q_hbm.at[pl.ds(ahead, q_ref.shape[0])], q_ref, sem)

    @pl.when(g == 0)
    def _():
        fetch.start()

    state = jnp.zeros((D, D), f32)
    for b in range(count // BLOCK):
        at = slice(b * BLOCK, (b + 1) * BLOCK)
        before_ref[b] = state
        k = k_ref[at, :]
        fh, fl = split(jnp.tanh(k))
        vv = lanes(*split(v_ref[at, :]))
        kp_ref[at, :] = lanes(*split(k * SCORE_SCALE), fh, fl)
        vp_ref[at, :] = vv
        state = state + halves(dot(rows(fh, fl), rows(vv, vv), TN))
    total_ref[...] = state
    tail_ref[:BLOCK] = k_ref[count - BLOCK :, :]
    tail_ref[BLOCK:] = v_ref[count - BLOCK :, :]

    @pl.when(g == pl.num_programs(0) - 1)
    def _():
        fetch.wait()


def local_states(queries, keys, values, ahead):
    count, width = keys.shape
    kv, nb = width // D, count // BLOCK
    one = pl.Squeezed()
    whole = lambda *shape: pl.BlockSpec((one, *shape), lambda g: (g,) + (0,) * len(shape))
    q_shape = (STEP * BLOCK, queries.shape[1])
    return pl.pallas_call(
        functools.partial(state_body, ahead=ahead * STEP * BLOCK),
        grid=(kv,),
        in_specs=[pl.BlockSpec((count, D), lambda g: (0, g))] * 2
        + [pl.BlockSpec(memory_space=pl.ANY)],
        out_specs=[
            whole(nb, D, D),
            whole(D, D),
            whole(2 * BLOCK, D),
            whole(count, 4 * D),
            whole(count, 2 * D),
            pl.BlockSpec(q_shape, lambda g: (0, 0)),
        ],
        out_shape=[
            pltpu.VMEM((kv, nb, D, D), f32),
            pltpu.VMEM((kv, D, D), f32),
            pltpu.VMEM((kv, 2 * BLOCK, D), f32),
            pltpu.VMEM((kv, count, 4 * D), bf),
            pltpu.VMEM((kv, count, 2 * D), bf),
            pltpu.VMEM(q_shape, f32),
        ],
        scratch_shapes=[pltpu.SemaphoreType.DMA(())],
        compiler_params=params(4),
        name="local_states",
    )(keys, values, queries)


def place():
    i = lax.axis_index("seq")
    return i // 8, (i // 2) % 4, i % 2


def chip_body(own_ref, other_ref, out_ref):
    core = place()[2]
    out_ref[...] = own_ref[core] + other_ref[core]


def row_body(own_ref, one_ref, two_ref, three_ref, sum_ref, before_ref):
    x = place()[1]
    got = [one_ref[...], two_ref[...], three_ref[...]]
    sum_ref[...] = own_ref[...] + got[0] + got[1] + got[2]
    before = jnp.zeros((D, D), f32)
    for by, state in enumerate(got, 1):
        before = before + jnp.where(x >= by, state, 0.0)
    before_ref[...] = before


def small_call(body, outs, name, *args):
    shape = jax.ShapeDtypeStruct((D, D), f32)
    return pl.pallas_call(
        body,
        out_shape=[shape] * outs,
        compiler_params=pltpu.CompilerParams(vmem_limit_bytes=2 << 20),
        name=name,
    )(*args)


def block_body(piece, ahead, carried, *refs):
    q_ref, kp_ref, vp_ref, *refs = refs
    if piece == 0:
        halo_ref, *refs = refs
    if ahead is not None:
        q_hbm, *refs = refs
    win_ref, lin_ref, fq_ref, *refs = refs[carried:]
    kv = kp_ref.shape[0]
    if ahead is not None:
        next_ref, sem = refs
        fetch = pltpu.make_async_copy(
            q_hbm.at[pl.ds(ahead * STEP * BLOCK, STEP * BLOCK)], next_ref, sem
        )
        fetch.start()
    row = lax.broadcasted_iota(jnp.int32, (BLOCK, BLOCK), 0)
    col = lax.broadcasted_iota(jnp.int32, (BLOCK, BLOCK), 1)
    own = rows(*[row >= col] * G)
    zero = jnp.zeros((BLOCK * G, BLOCK), bf)
    for j in range(STEP):
        block = piece * STEP + j
        tokens = slice(j * BLOCK, (j + 1) * BLOCK)
        here = slice(block * BLOCK, (block + 1) * BLOCK)
        there = slice((block - 1) * BLOCK, block * BLOCK)
        for g in range(kv):
            kh, kl = kp_ref[g, here, :D], kp_ref[g, here, D : 2 * D]
            fh, fl = kp_ref[g, here, 2 * D : 3 * D], kp_ref[g, here, 3 * D :]
            v_own = vp_ref[g, here, :]
            if block:
                ph, pl_ = kp_ref[g, there, :D], kp_ref[g, there, D : 2 * D]
                v_prior = vp_ref[g, there, :]
            else:
                ph, pl_ = split(halo_ref[g, :BLOCK] * SCORE_SCALE)
                v_prior = lanes(*split(halo_ref[g, BLOCK:]))
            kk = rows(lanes(kh, kh, kl, kl), lanes(ph, ph, pl_, pl_))
            ff = rows(lanes(fh, fh), lanes(fl, fl))
            v_both = rows(v_own, v_prior)
            heads = [slice(i * D, (i + 1) * D) for i in range(g * G, (g + 1) * G)]
            q = rows(*[q_ref[tokens, at] for at in heads])
            qh, ql = split(q)
            s = dot(lanes(qh, ql, qh, ql), kk, NT)
            f2 = lanes(*split(jnp.tanh(q)))
            fq_ref[j, g * G * BLOCK : (g + 1) * G * BLOCK, :] = f2
            a = jnp.where(own, halves(dot(f2, ff, NT)), 0.0)
            lin = halves(dot(lanes(*split(a)), rows(v_own, v_own)))
            before = s[:, BLOCK:]
            if block == 0:
                before = jnp.where(lax.axis_index("seq") > 0, before, -1e30)
            t = jnp.where(own, s[:, :BLOCK], before)
            p = jnp.exp2(t - jnp.max(t, axis=1, keepdims=True))
            total = jnp.sum(p, axis=1, keepdims=True)
            wh, wl = split(p)
            p4 = lanes(
                jnp.where(own, wh, zero),
                jnp.where(own, zero, wh),
                jnp.where(own, wl, zero),
                jnp.where(own, zero, wl),
            )
            win = halves(dot(p4, rows(v_both, v_both))) * (1.0 / total)
            for i, at in enumerate(heads):
                win_ref[tokens, at] = win[i * BLOCK : (i + 1) * BLOCK]
                lin_ref[tokens, at] = lin[i * BLOCK : (i + 1) * BLOCK]
    if ahead is not None:
        fetch.wait()


def block_part(piece, q, kp, vp, made, ahead=None, queries=None, halo=None):
    kv, count, _ = kp.shape
    nb = count // BLOCK
    width = q.shape[1]
    whole = lambda x: pl.BlockSpec(x.shape, lambda _: (0,) * x.ndim)
    args = [q, kp, vp]
    if halo is not None:
        args.append(halo)
    specs = [whole(x) for x in args]
    if ahead is not None:
        args.append(queries)
        specs.append(pl.BlockSpec(memory_space=pl.ANY))
    aliases = {len(args) + i: i for i in range(len(made))}
    big = pl.BlockSpec((STEP * BLOCK, width), lambda _: (piece, 0))
    out_specs = [big, big, pl.BlockSpec((STEP, kv * G * BLOCK, 2 * D), lambda _: (piece, 0, 0))]
    out_shape = [
        pltpu.VMEM((count, width), f32),
        pltpu.VMEM((count, width), f32),
        pltpu.VMEM((nb, kv * G * BLOCK, 2 * D), bf),
    ]
    scratch = []
    if ahead is not None:
        out_specs.append(whole(q))
        out_shape.append(pltpu.VMEM(q.shape, f32))
        scratch.append(pltpu.SemaphoreType.DMA(()))
    return pl.pallas_call(
        lambda *refs: block_body(piece, ahead, len(made), *refs),
        grid=(1,),
        in_specs=specs + [pl.BlockSpec(memory_space=pl.ANY)] * len(made),
        out_specs=out_specs,
        out_shape=out_shape,
        scratch_shapes=scratch,
        input_output_aliases=aliases,
        compiler_params=params(6),
        name=f"blocks_{piece}",
    )(*args, *made)


def linear_body(fq_ref, part_ref, inner_ref, mine_ref, their_ref, other_ref, lin_ref, sq_ref):
    core = place()[2]
    for j in range(STEP):
        tokens = slice(j * BLOCK, (j + 1) * BLOCK)
        sq = jnp.zeros((BLOCK, D), f32)
        for g in range(other_ref.shape[0]):
            state = jnp.where(core == g, mine_ref[...], their_ref[...])
            state = state + jnp.where(core == 1, other_ref[g], 0.0) + inner_ref[g, j]
            ss = lanes(*split(state))
            fq = fq_ref[j, g * G * BLOCK : (g + 1) * G * BLOCK, :]
            lin = halves(dot(fq, rows(ss, ss)))
            for i in range(G):
                at = slice((g * G + i) * D, (g * G + i + 1) * D)
                x = lin[i * BLOCK : (i + 1) * BLOCK] + part_ref[tokens, at]
                lin_ref[tokens, at] = x
                sq = sq + x * x
        sq_ref[j] = jnp.sum(sq.T, axis=0, keepdims=True)


def linear_part(fq, part, inner, mine, theirs, other):
    count, width = part.shape
    kv, nb = inner.shape[:2]
    big = pl.BlockSpec((STEP * BLOCK, width), lambda b: (b, 0))
    state = pl.BlockSpec((D, D), lambda b: (0, 0))
    return pl.pallas_call(
        linear_body,
        grid=(nb // STEP,),
        in_specs=[
            pl.BlockSpec((STEP,) + fq.shape[1:], lambda b: (b, 0, 0)),
            big,
            pl.BlockSpec((kv, STEP, D, D), lambda b: (0, b, 0, 0)),
            state,
            state,
            pl.BlockSpec((kv, D, D), lambda b: (0, 0, 0)),
        ],
        out_specs=[big, pl.BlockSpec((STEP, 1, BLOCK), lambda b: (b, 0, 0))],
        out_shape=[
            pltpu.VMEM((count, width), f32),
            pltpu.VMEM((nb, 1, BLOCK), f32),
        ],
        compiler_params=params(4),
        name="linear",
    )(fq, part, inner, mine, theirs, other)


def combine_body(lin_ref, win_ref, sa_ref, sb_ref, gain_ref, out_ref):
    for r in range(lin_ref.shape[0] // BLOCK):
        ms = (sa_ref[r] + sb_ref[r]) * (1.0 / (QUERY_HEADS * D))
        inv = jnp.broadcast_to(lax.rsqrt(ms + EPS), (BLOCK, BLOCK)).T
        row = slice(r * BLOCK, (r + 1) * BLOCK)
        for i in range(lin_ref.shape[1] // D):
            at = slice(i * D, (i + 1) * D)
            out_ref[row, at] = lin_ref[row, at] * inv * gain_ref[:, at] + win_ref[row, at]


def combine(lin, win, sa, sb, gain):
    count, width = lin.shape
    n = 2
    big = pl.BlockSpec((n * BLOCK, width), lambda j: (j, 0))
    small = pl.BlockSpec((n, 1, BLOCK), lambda j: (j, 0, 0))
    return pl.pallas_call(
        combine_body,
        grid=(count // (n * BLOCK),),
        in_specs=[big, big, small, small, pl.BlockSpec((1, width), lambda j: (0, 0))],
        out_specs=big,
        out_shape=jax.ShapeDtypeStruct((count, width), f32),
        compiler_params=params(6),
        name="combine",
    )(lin, win, sa, sb, gain)


def shift_x(by):
    return [(i, i // 8 * 8 + (i + 2 * by) % 8) for i in range(32)]


def down_from(y):
    return [(y * 8 + i, (y + 1) * 8 + i) for i in range(8)]


SWAP = [(i, i ^ 1) for i in range(32)]


def shards(queries, keys, values, gain):
    count = queries.shape[0]
    nb = count // BLOCK
    heads = lax.axis_size("head")
    assert heads == 4 and nb == 8 and lax.axis_size("seq") == 32
    queries, keys, values = (
        pltpu.with_memory_space_constraint(x, pltpu.HBM) for x in (queries, keys, values)
    )

    def move(x, pairs):
        return lax.ppermute(x, "seq", pairs)

    def tie(*xs):
        return lax.optimization_barrier(xs)

    order = (1, 2, 3, 0)
    inner, total, tail, kp, vp, q = local_states(queries, keys, values, order[0])
    other = move(total, SWAP)
    (chip,) = small_call(chip_body, 1, "chip_sum", total, other)
    along_x = [move(chip, shift_x(by)) for by in (1, 2, 3)]
    halo = move(tail, [(i, i + 1) for i in range(31)])
    *made, q = block_part(order[0], q, kp, vp, (), order[1], queries)
    *made, one, two, three = tie(*made, *along_x)
    row, mine = small_call(row_body, 2, "row_sum", chip, one, two, three)
    for y in range(3):
        got = move(row, down_from(y))
        *made, mine = tie(*made, mine)
        if y < 2:
            *made, q = block_part(order[y + 1], q, kp, vp, made, order[y + 2], queries)
        else:
            made = block_part(0, q, kp, vp, made, halo=halo)
        *made, got = tie(*made, got)
        row, mine = row + got, mine + got
    theirs = move(mine, SWAP)
    win, part, fq = made
    lin, sq = linear_part(fq, part, inner, mine, theirs, other)
    sq = sq + lax.ppermute(sq, "head", [(i, i ^ 1) for i in range(heads)])
    across = lax.ppermute(sq, "head", [(i, heads - 1 - i) for i in range(heads)])
    return combine(lin, win, sq, across, gain[None, :])


def solution(mesh):
    in_specs = (P("seq", "head"), P("seq", "head"), P("seq", "head"), P("head"))
    return jax.shard_map(
        shards, mesh=mesh, in_specs=in_specs, out_specs=P("seq", "head"), check_vma=False
    )
```

```python
import functools
import math

import jax
import jax.numpy as jnp
from jax import lax
from jax.experimental import pallas as pl
from jax.experimental.pallas import tpu as pltpu
from jax.sharding import PartitionSpec as P

QUERY_HEADS = 64
KEY_VALUE_HEADS = 8
D = 128
G = QUERY_HEADS // KEY_VALUE_HEADS
BLOCK = 128
STEP = 2
WIDE = 4
EPS = 1e-6
SCORE_SCALE = math.log2(math.e) / math.sqrt(D)

f32 = jnp.float32
bf = jnp.bfloat16
NT = (((1,), (1,)), ((), ()))
TN = (((0,), (0,)), ((), ()))


def split(x):
    hi = x.astype(bf)
    return hi, (x - hi.astype(f32)).astype(bf)


def lanes(*xs):
    return jnp.concatenate(xs, axis=1)


def rows(*xs):
    return jnp.concatenate(xs, axis=0)


def dot(a, b, dims=(((1,), (0,)), ((), ()))):
    return lax.dot_general(a, b, dims, preferred_element_type=f32)


def halves(x):
    return x[:, :D] + x[:, D:]


def params(mib):
    return pltpu.CompilerParams(
        vmem_limit_bytes=mib << 20, dimension_semantics=("arbitrary",)
    )


def state_body(
    k_ref, v_ref, q_hbm, before_ref, total_ref, tail_ref, kp_ref, vp_ref, q_ref, sems, *, ahead
):
    count = k_ref.shape[0]
    g = pl.program_id(0)

    def fetch(j):
        to = pl.ds(pl.multiple_of(j * BLOCK, BLOCK), BLOCK)
        at = pl.ds(pl.multiple_of((ahead * STEP + j) * BLOCK, BLOCK), BLOCK)
        return pltpu.make_async_copy(q_hbm.at[at], q_ref.at[to], sems.at[j])

    @pl.when(g == 0)
    def _():
        @pl.loop(0, STEP)
        def _(j):
            fetch(j).start()

    state = jnp.zeros((D, D), f32)
    for b in range(count // BLOCK):
        at = slice(b * BLOCK, (b + 1) * BLOCK)
        before_ref[b] = state
        k = k_ref[at, :]
        fh, fl = split(jnp.tanh(k))
        vv = lanes(*split(v_ref[at, :]))
        kp_ref[at, :] = lanes(*split(k * SCORE_SCALE), fh, fl)
        vp_ref[at, :] = vv
        state = state + halves(dot(rows(fh, fl), rows(vv, vv), TN))
    total_ref[...] = state
    tail_ref[:BLOCK] = k_ref[count - BLOCK :, :]
    tail_ref[BLOCK:] = v_ref[count - BLOCK :, :]

    @pl.when(g == pl.num_programs(0) - 1)
    def _():
        for j in range(STEP):
            fetch(j).wait()


def local_states(queries, keys, values, ahead):
    count, width = keys.shape
    kv, nb = width // D, count // BLOCK
    one = pl.Squeezed()
    whole = lambda *shape: pl.BlockSpec((one, *shape), lambda g: (g,) + (0,) * len(shape))
    q_shape = (STEP * BLOCK, queries.shape[1])
    return pl.pallas_call(
        functools.partial(state_body, ahead=ahead),
        grid=(kv,),
        in_specs=[pl.BlockSpec((count, D), lambda g: (0, g))] * 2
        + [pl.BlockSpec(memory_space=pl.ANY)],
        out_specs=[
            whole(nb, D, D),
            whole(D, D),
            whole(2 * BLOCK, D),
            whole(count, 4 * D),
            whole(count, 2 * D),
            pl.BlockSpec(memory_space=pl.ANY),
        ],
        out_shape=[
            pltpu.VMEM((kv, nb, D, D), f32),
            pltpu.VMEM((kv, D, D), f32),
            pltpu.VMEM((kv, 2 * BLOCK, D), f32),
            pltpu.VMEM((kv, count, 4 * D), bf),
            pltpu.VMEM((kv, count, 2 * D), bf),
            pltpu.VMEM(q_shape, f32),
        ],
        scratch_shapes=[pltpu.SemaphoreType.DMA((STEP,))],
        compiler_params=params(4),
        name="local_states",
    )(keys, values, queries)


def place():
    i = lax.axis_index("seq")
    return i // 8, (i // 2) % 4, i % 2


def chip_body(own_ref, other_ref, out_ref):
    core = place()[2]
    out_ref[...] = own_ref[core] + other_ref[core]


def row_body(own_ref, one_ref, two_ref, three_ref, sum_ref, before_ref):
    x = place()[1]
    got = [one_ref[...], two_ref[...], three_ref[...]]
    sum_ref[...] = own_ref[...] + got[0] + got[1] + got[2]
    before = jnp.zeros((D, D), f32)
    for by, state in enumerate(got, 1):
        before = before + jnp.where(x >= by, state, 0.0)
    before_ref[...] = before


def small_call(body, outs, name, *args):
    shape = jax.ShapeDtypeStruct((D, D), f32)
    return pl.pallas_call(
        body,
        out_shape=[shape] * outs,
        compiler_params=pltpu.CompilerParams(vmem_limit_bytes=2 << 20),
        name=name,
    )(*args)


def block_body(piece, ahead, carried, *refs):
    q_ref, kp_ref, vp_ref, *refs = refs
    if piece == 0:
        halo_ref, *refs = refs
    if ahead is not None:
        q_hbm, *refs = refs
    win_ref, lin_ref, fq_ref, *refs = refs[carried:]
    kv = kp_ref.shape[0]
    if ahead is not None:
        next_ref, sems = refs

        def fetch(j):
            to = pl.ds(pl.multiple_of(j * BLOCK, BLOCK), BLOCK)
            at = pl.ds(pl.multiple_of((ahead * STEP + j) * BLOCK, BLOCK), BLOCK)
            return pltpu.make_async_copy(q_hbm.at[at], next_ref.at[to], sems.at[j])

        @pl.loop(0, STEP)
        def _(j):
            fetch(j).start()

    row = lax.broadcasted_iota(jnp.int32, (BLOCK, BLOCK), 0)
    col = lax.broadcasted_iota(jnp.int32, (BLOCK, BLOCK), 1)
    own = rows(*[row >= col] * G)
    zero = jnp.zeros((BLOCK * G, BLOCK), bf)
    for j in range(STEP):
        block = piece * STEP + j
        tokens = slice(j * BLOCK, (j + 1) * BLOCK)
        here = slice(block * BLOCK, (block + 1) * BLOCK)
        there = slice((block - 1) * BLOCK, block * BLOCK)
        for g in range(kv):
            kh, kl = kp_ref[g, here, :D], kp_ref[g, here, D : 2 * D]
            fh, fl = kp_ref[g, here, 2 * D : 3 * D], kp_ref[g, here, 3 * D :]
            v_own = vp_ref[g, here, :]
            if block:
                ph, pl_ = kp_ref[g, there, :D], kp_ref[g, there, D : 2 * D]
                v_prior = vp_ref[g, there, :]
            else:
                ph, pl_ = split(halo_ref[g, :BLOCK] * SCORE_SCALE)
                v_prior = lanes(*split(halo_ref[g, BLOCK:]))
            kk = rows(lanes(kh, kh, kl, kl), lanes(ph, ph, pl_, pl_))
            ff = rows(lanes(fh, fh), lanes(fl, fl))
            v_both = rows(v_own, v_prior)
            heads = [slice(i * D, (i + 1) * D) for i in range(g * G, (g + 1) * G)]
            q = rows(*[q_ref[tokens, at] for at in heads])
            qh, ql = split(q)
            s = dot(lanes(qh, ql, qh, ql), kk, NT)
            f2 = lanes(*split(jnp.tanh(q)))
            fq_ref[j, g * G * BLOCK : (g + 1) * G * BLOCK, :] = f2
            a = jnp.where(own, halves(dot(f2, ff, NT)), 0.0)
            lin = halves(dot(lanes(*split(a)), rows(v_own, v_own)))
            before = s[:, BLOCK:]
            if block == 0:
                before = jnp.where(lax.axis_index("seq") > 0, before, -1e30)
            t = jnp.where(own, s[:, :BLOCK], before)
            p = jnp.exp2(t - jnp.max(t, axis=1, keepdims=True))
            total = jnp.sum(p, axis=1, keepdims=True)
            wh, wl = split(p)
            p4 = lanes(
                jnp.where(own, wh, zero),
                jnp.where(own, zero, wh),
                jnp.where(own, wl, zero),
                jnp.where(own, zero, wl),
            )
            win = halves(dot(p4, rows(v_both, v_both))) * (1.0 / total)
            for i, at in enumerate(heads):
                win_ref[tokens, at] = win[i * BLOCK : (i + 1) * BLOCK]
                lin_ref[tokens, at] = lin[i * BLOCK : (i + 1) * BLOCK]
    if ahead is not None:
        for j in range(STEP):
            fetch(j).wait()


def block_part(piece, q, kp, vp, made, ahead=None, queries=None, halo=None):
    kv, count, _ = kp.shape
    nb = count // BLOCK
    width = q.shape[1]
    whole = lambda x: pl.BlockSpec(x.shape, lambda _: (0,) * x.ndim)
    args = [q, kp, vp]
    if halo is not None:
        args.append(halo)
    specs = [whole(x) for x in args]
    if ahead is not None:
        args.append(queries)
        specs.append(pl.BlockSpec(memory_space=pl.ANY))
    aliases = {len(args) + i: i for i in range(len(made))}
    big = pl.BlockSpec((STEP * BLOCK, width), lambda _: (piece, 0))
    out_specs = [big, big, pl.BlockSpec((STEP, kv * G * BLOCK, 2 * D), lambda _: (piece, 0, 0))]
    out_shape = [
        pltpu.VMEM((count, width), f32),
        pltpu.VMEM((count, width), f32),
        pltpu.VMEM((nb, kv * G * BLOCK, 2 * D), bf),
    ]
    scratch = []
    if ahead is not None:
        out_specs.append(pl.BlockSpec(memory_space=pl.ANY))
        out_shape.append(pltpu.VMEM(q.shape, f32))
        scratch.append(pltpu.SemaphoreType.DMA((STEP,)))
    return pl.pallas_call(
        lambda *refs: block_body(piece, ahead, len(made), *refs),
        grid=(1,),
        in_specs=specs + [pl.BlockSpec(memory_space=pl.ANY)] * len(made),
        out_specs=out_specs,
        out_shape=out_shape,
        scratch_shapes=scratch,
        input_output_aliases=aliases,
        compiler_params=params(6),
        name=f"blocks_{piece}",
    )(*args, *made)


def linear_body(fq_ref, part_ref, inner_ref, mine_ref, their_ref, other_ref, lin_ref, sq_ref):
    core = place()[2]
    for j in range(WIDE):
        tokens = slice(j * BLOCK, (j + 1) * BLOCK)
        sq = jnp.zeros((BLOCK, D), f32)
        for g in range(other_ref.shape[0]):
            state = jnp.where(core == g, mine_ref[...], their_ref[...])
            state = state + jnp.where(core == 1, other_ref[g], 0.0) + inner_ref[g, j]
            ss = lanes(*split(state))
            fq = fq_ref[j, g * G * BLOCK : (g + 1) * G * BLOCK, :]
            lin = halves(dot(fq, rows(ss, ss)))
            for i in range(G):
                at = slice((g * G + i) * D, (g * G + i + 1) * D)
                x = lin[i * BLOCK : (i + 1) * BLOCK] + part_ref[tokens, at]
                lin_ref[tokens, at] = x
                sq = sq + x * x
        sq_ref[j] = jnp.sum(sq.T, axis=0, keepdims=True)


def linear_part(fq, part, inner, mine, theirs, other):
    count, width = part.shape
    kv, nb = inner.shape[:2]
    big = pl.BlockSpec((WIDE * BLOCK, width), lambda b: (b, 0))
    state = pl.BlockSpec((D, D), lambda b: (0, 0))
    return pl.pallas_call(
        linear_body,
        grid=(nb // WIDE,),
        in_specs=[
            pl.BlockSpec((WIDE,) + fq.shape[1:], lambda b: (b, 0, 0)),
            big,
            pl.BlockSpec((kv, WIDE, D, D), lambda b: (0, b, 0, 0)),
            state,
            state,
            pl.BlockSpec((kv, D, D), lambda b: (0, 0, 0)),
        ],
        out_specs=[big, pl.BlockSpec((WIDE, 1, BLOCK), lambda b: (b, 0, 0))],
        out_shape=[
            pltpu.VMEM((count, width), f32),
            pltpu.VMEM((nb, 1, BLOCK), f32),
        ],
        compiler_params=params(6),
        name="linear",
    )(fq, part, inner, mine, theirs, other)


def combine_body(lin_ref, win_ref, s0, s1, s2, s3, gain_ref, out_hbm, out_ref, sems):
    def send(b):
        row = pl.ds(pl.multiple_of(b * BLOCK, BLOCK), BLOCK)
        return row, pltpu.make_async_copy(out_ref.at[row], out_hbm.at[row], sems.at[b])

    @pl.loop(0, s0.shape[0])
    def _(b):
        ms = ((s0[b] + s1[b]) + (s2[b] + s3[b])) * (1.0 / (QUERY_HEADS * D))
        inv = jnp.broadcast_to(lax.rsqrt(ms + EPS), (BLOCK, BLOCK)).T
        row, copy = send(b)
        for i in range(lin_ref.shape[1] // D):
            at = slice(i * D, (i + 1) * D)
            out_ref[row, at] = lin_ref[row, at] * inv * gain_ref[:, at] + win_ref[row, at]
        copy.start()

    @pl.loop(0, s0.shape[0])
    def _(b):
        send(b)[1].wait()


def combine(lin, win, squares, gain):
    args = [lin, win, *squares, gain]
    return pl.pallas_call(
        combine_body,
        grid=(1,),
        in_specs=[pl.BlockSpec(x.shape, lambda _, x=x: (0,) * x.ndim) for x in args],
        out_specs=pl.BlockSpec(memory_space=pl.ANY),
        out_shape=pltpu.HBM(lin.shape, f32),
        scratch_shapes=[
            pltpu.VMEM(lin.shape, f32),
            pltpu.SemaphoreType.DMA((squares[0].shape[0],)),
        ],
        compiler_params=params(10),
        name="combine",
    )(*args)


def shift_x(by):
    return [(i, i // 8 * 8 + (i + 2 * by) % 8) for i in range(32)]


def down_from(y):
    return [(y * 8 + i, (y + 1) * 8 + i) for i in range(8)]


SWAP = [(i, i ^ 1) for i in range(32)]


def shards(queries, keys, values, gain):
    count = queries.shape[0]
    nb = count // BLOCK
    heads = lax.axis_size("head")
    assert heads == 4 and nb == 8 and lax.axis_size("seq") == 32
    queries, keys, values = (
        pltpu.with_memory_space_constraint(x, pltpu.HBM) for x in (queries, keys, values)
    )

    def move(x, pairs):
        return lax.ppermute(x, "seq", pairs)

    def tie(*xs):
        return lax.optimization_barrier(xs)

    order = (1, 2, 3, 0)
    inner, total, tail, kp, vp, q = local_states(queries, keys, values, order[0])
    other = move(total, SWAP)
    (chip,) = small_call(chip_body, 1, "chip_sum", total, other)
    along_x = [move(chip, shift_x(by)) for by in (1, 2, 3)]
    halo = move(tail, [(i, i + 1) for i in range(31)])
    *made, q = block_part(order[0], q, kp, vp, (), order[1], queries)
    *made, one, two, three = tie(*made, *along_x)
    row, mine = small_call(row_body, 2, "row_sum", chip, one, two, three)
    for y in range(3):
        got = move(row, down_from(y))
        *made, mine = tie(*made, mine)
        if y < 2:
            *made, q = block_part(order[y + 1], q, kp, vp, made, order[y + 2], queries)
        else:
            made = block_part(0, q, kp, vp, made, halo=halo)
        *made, got = tie(*made, got)
        row, mine = row + got, mine + got
    theirs = move(mine, SWAP)
    win, part, fq = made
    lin, sq = linear_part(fq, part, inner, mine, theirs, other)
    squares = [sq]
    for by in range(1, heads):
        squares.append(lax.ppermute(sq, "head", [(i, (i + by) % heads) for i in range(heads)]))
    return combine(lin, win, squares, gain[None, :])


def solution(mesh):
    in_specs = (P("seq", "head"), P("seq", "head"), P("seq", "head"), P("head"))
    return jax.shard_map(
        shards, mesh=mesh, in_specs=in_specs, out_specs=P("seq", "head"), check_vma=False
    )
```

```python
import functools
import math

import jax
import jax.numpy as jnp
from jax import lax
from jax.experimental import pallas as pl
from jax.experimental.pallas import tpu as pltpu
from jax.sharding import PartitionSpec as P


QUERY_HEADS = 64
KEY_VALUE_HEADS = 8
D = 128
G = QUERY_HEADS // KEY_VALUE_HEADS
BLOCK = 128
STEP = 2
WIDE = 4
EPS = 1e-6
SCORE_SCALE = math.log2(math.e) / math.sqrt(D)

f32 = jnp.float32
bf = jnp.bfloat16
NT = (((1,), (1,)), ((), ()))
TN = (((0,), (0,)), ((), ()))


def split(x):
    hi = x.astype(bf)
    return hi, (x - hi.astype(f32)).astype(bf)


def lanes(*xs):
    return jnp.concatenate(xs, axis=1)


def rows(*xs):
    return jnp.concatenate(xs, axis=0)


def dot(a, b, dims=(((1,), (0,)), ((), ()))):
    return lax.dot_general(a, b, dims, preferred_element_type=f32)


def halves(x):
    return x[:, :D] + x[:, D:]


def params(mib):
    return pltpu.CompilerParams(
        vmem_limit_bytes=mib << 20, dimension_semantics=("arbitrary",)
    )


def state_body(
    k_ref, v_ref, q_hbm, before_ref, total_ref, tail_ref, kp_ref, vp_ref, q_ref, sems, *, ahead
):
    count = k_ref.shape[0]
    g = pl.program_id(0)

    def fetch(j):
        to = pl.ds(pl.multiple_of(j * BLOCK, BLOCK), BLOCK)
        at = pl.ds(pl.multiple_of((ahead * STEP + j) * BLOCK, BLOCK), BLOCK)
        return pltpu.make_async_copy(q_hbm.at[at], q_ref.at[to], sems.at[j])

    @pl.when(g == 0)
    def _():
        @pl.loop(0, STEP)
        def _(j):
            fetch(j).start()

    state = jnp.zeros((D, D), f32)
    for b in range(count // BLOCK):
        at = slice(b * BLOCK, (b + 1) * BLOCK)
        before_ref[b] = state
        k = k_ref[at, :]
        fh, fl = split(jnp.tanh(k))
        vv = lanes(*split(v_ref[at, :]))
        kp_ref[at, :] = lanes(*split(k * SCORE_SCALE), fh, fl)
        vp_ref[at, :] = vv
        state = state + halves(dot(rows(fh, fl), rows(vv, vv), TN))
    total_ref[...] = state
    tail_ref[:BLOCK] = k_ref[count - BLOCK :, :]
    tail_ref[BLOCK:] = v_ref[count - BLOCK :, :]

    @pl.when(g == pl.num_programs(0) - 1)
    def _():
        for j in range(STEP):
            fetch(j).wait()


def local_states(queries, keys, values, ahead):
    count, width = keys.shape
    kv, nb = width // D, count // BLOCK
    one = pl.Squeezed()
    whole = lambda *shape: pl.BlockSpec((one, *shape), lambda g: (g,) + (0,) * len(shape))
    q_shape = (STEP * BLOCK, queries.shape[1])
    return pl.pallas_call(
        functools.partial(state_body, ahead=ahead),
        grid=(kv,),
        in_specs=[pl.BlockSpec((count, D), lambda g: (0, g))] * 2
        + [pl.BlockSpec(memory_space=pl.ANY)],
        out_specs=[
            whole(nb, D, D),
            whole(D, D),
            whole(2 * BLOCK, D),
            whole(count, 4 * D),
            whole(count, 2 * D),
            pl.BlockSpec(memory_space=pl.ANY),
        ],
        out_shape=[
            pltpu.VMEM((kv, nb, D, D), f32),
            pltpu.VMEM((kv, D, D), f32),
            pltpu.VMEM((kv, 2 * BLOCK, D), f32),
            pltpu.VMEM((kv, count, 4 * D), bf),
            pltpu.VMEM((kv, count, 2 * D), bf),
            pltpu.VMEM(q_shape, f32),
        ],
        scratch_shapes=[pltpu.SemaphoreType.DMA((STEP,))],
        compiler_params=params(4),
        name="local_states",
    )(keys, values, queries)


def place():
    i = lax.axis_index("seq")
    return i // 8, (i // 2) % 4, i % 2


def chip_body(own_ref, other_ref, out_ref):
    core = place()[2]
    out_ref[...] = own_ref[core] + other_ref[core]


def row_body(own_ref, one_ref, two_ref, three_ref, sum_ref, before_ref):
    x = place()[1]
    got = [one_ref[...], two_ref[...], three_ref[...]]
    sum_ref[...] = own_ref[...] + got[0] + got[1] + got[2]
    before = jnp.zeros((D, D), f32)
    for by, state in enumerate(got, 1):
        before = before + jnp.where(x >= by, state, 0.0)
    before_ref[...] = before


def small_call(body, outs, *args):
    shape = jax.ShapeDtypeStruct((D, D), f32)
    return pl.pallas_call(
        body,
        out_shape=[shape] * outs,
        compiler_params=pltpu.CompilerParams(vmem_limit_bytes=2 << 20),
    )(*args)


def block_body(piece, ahead, carried, *refs):
    q_ref, kp_ref, vp_ref, *refs = refs
    if piece == 0:
        halo_ref, *refs = refs
    if ahead is not None:
        q_hbm, *refs = refs
    win_ref, lin_ref, fq_ref, *refs = refs[carried:]
    kv = kp_ref.shape[0]
    if ahead is not None:
        next_ref, sems = refs

        def fetch(j):
            to = pl.ds(pl.multiple_of(j * BLOCK, BLOCK), BLOCK)
            at = pl.ds(pl.multiple_of((ahead * STEP + j) * BLOCK, BLOCK), BLOCK)
            return pltpu.make_async_copy(q_hbm.at[at], next_ref.at[to], sems.at[j])

        @pl.loop(0, STEP)
        def _(j):
            fetch(j).start()

    row = lax.broadcasted_iota(jnp.int32, (BLOCK, BLOCK), 0)
    col = lax.broadcasted_iota(jnp.int32, (BLOCK, BLOCK), 1)
    own = rows(*[row >= col] * G)
    zero = jnp.zeros((BLOCK * G, BLOCK), bf)
    for j in range(STEP):
        block = piece * STEP + j
        tokens = slice(j * BLOCK, (j + 1) * BLOCK)
        here = slice(block * BLOCK, (block + 1) * BLOCK)
        there = slice((block - 1) * BLOCK, block * BLOCK)
        for g in range(kv):
            kh, kl = kp_ref[g, here, :D], kp_ref[g, here, D : 2 * D]
            fh, fl = kp_ref[g, here, 2 * D : 3 * D], kp_ref[g, here, 3 * D :]
            v_own = vp_ref[g, here, :]
            if block:
                ph, pl_ = kp_ref[g, there, :D], kp_ref[g, there, D : 2 * D]
                v_prior = vp_ref[g, there, :]
            else:
                ph, pl_ = split(halo_ref[g, :BLOCK] * SCORE_SCALE)
                v_prior = lanes(*split(halo_ref[g, BLOCK:]))
            kk = rows(lanes(kh, kh, kl, kl), lanes(ph, ph, pl_, pl_))
            ff = rows(lanes(fh, fh), lanes(fl, fl))
            v_both = rows(v_own, v_prior)
            heads = [slice(i * D, (i + 1) * D) for i in range(g * G, (g + 1) * G)]
            q = rows(*[q_ref[tokens, at] for at in heads])
            qh, ql = split(q)
            s = dot(lanes(qh, ql, qh, ql), kk, NT)
            f2 = lanes(*split(jnp.tanh(q)))
            fq_ref[j, g * G * BLOCK : (g + 1) * G * BLOCK, :] = f2
            a = jnp.where(own, halves(dot(f2, ff, NT)), 0.0)
            lin = halves(dot(lanes(*split(a)), rows(v_own, v_own)))
            before = s[:, BLOCK:]
            if block == 0:
                before = jnp.where(lax.axis_index("seq") > 0, before, -1e30)
            t = jnp.where(own, s[:, :BLOCK], before)
            p = jnp.exp2(t - jnp.max(t, axis=1, keepdims=True))
            total = jnp.sum(p, axis=1, keepdims=True)
            wh, wl = split(p)
            p4 = lanes(
                jnp.where(own, wh, zero),
                jnp.where(own, zero, wh),
                jnp.where(own, wl, zero),
                jnp.where(own, zero, wl),
            )
            win = halves(dot(p4, rows(v_both, v_both))) * (1.0 / total)
            for i, at in enumerate(heads):
                win_ref[tokens, at] = win[i * BLOCK : (i + 1) * BLOCK]
                lin_ref[tokens, at] = lin[i * BLOCK : (i + 1) * BLOCK]
    if ahead is not None:
        for j in range(STEP):
            fetch(j).wait()


def block_part(piece, q, kp, vp, made, ahead=None, queries=None, halo=None):
    kv, count, _ = kp.shape
    nb = count // BLOCK
    width = q.shape[1]
    whole = lambda x: pl.BlockSpec(x.shape, lambda _: (0,) * x.ndim)
    args = [q, kp, vp]
    if halo is not None:
        args.append(halo)
    specs = [whole(x) for x in args]
    if ahead is not None:
        args.append(queries)
        specs.append(pl.BlockSpec(memory_space=pl.ANY))
    aliases = {len(args) + i: i for i in range(len(made))}
    big = pl.BlockSpec((STEP * BLOCK, width), lambda _: (piece, 0))
    out_specs = [big, big, pl.BlockSpec((STEP, kv * G * BLOCK, 2 * D), lambda _: (piece, 0, 0))]
    out_shape = [
        pltpu.VMEM((count, width), f32),
        pltpu.VMEM((count, width), f32),
        pltpu.VMEM((nb, kv * G * BLOCK, 2 * D), bf),
    ]
    scratch = []
    if ahead is not None:
        out_specs.append(pl.BlockSpec(memory_space=pl.ANY))
        out_shape.append(pltpu.VMEM(q.shape, f32))
        scratch.append(pltpu.SemaphoreType.DMA((STEP,)))
    return pl.pallas_call(
        lambda *refs: block_body(piece, ahead, len(made), *refs),
        grid=(1,),
        in_specs=specs + [pl.BlockSpec(memory_space=pl.ANY)] * len(made),
        out_specs=out_specs,
        out_shape=out_shape,
        scratch_shapes=scratch,
        input_output_aliases=aliases,
        compiler_params=params(6),
    )(*args, *made)


def linear_body(fq_ref, part_ref, inner_ref, mine_ref, their_ref, other_ref, lin_ref, sq_ref):
    core = place()[2]
    for j in range(WIDE):
        tokens = slice(j * BLOCK, (j + 1) * BLOCK)
        sq = jnp.zeros((BLOCK, D), f32)
        for g in range(other_ref.shape[0]):
            state = jnp.where(core == g, mine_ref[...], their_ref[...])
            state = state + jnp.where(core == 1, other_ref[g], 0.0) + inner_ref[g, j]
            ss = lanes(*split(state))
            fq = fq_ref[j, g * G * BLOCK : (g + 1) * G * BLOCK, :]
            lin = halves(dot(fq, rows(ss, ss)))
            for i in range(G):
                at = slice((g * G + i) * D, (g * G + i + 1) * D)
                x = lin[i * BLOCK : (i + 1) * BLOCK] + part_ref[tokens, at]
                lin_ref[tokens, at] = x
                sq = sq + x * x
        sq_ref[j] = jnp.sum(sq.T, axis=0, keepdims=True)


def linear_part(fq, part, inner, mine, theirs, other):
    count, width = part.shape
    kv, nb = inner.shape[:2]
    big = pl.BlockSpec((WIDE * BLOCK, width), lambda b: (b, 0))
    state = pl.BlockSpec((D, D), lambda b: (0, 0))
    return pl.pallas_call(
        linear_body,
        grid=(nb // WIDE,),
        in_specs=[
            pl.BlockSpec((WIDE,) + fq.shape[1:], lambda b: (b, 0, 0)),
            big,
            pl.BlockSpec((kv, WIDE, D, D), lambda b: (0, b, 0, 0)),
            state,
            state,
            pl.BlockSpec((kv, D, D), lambda b: (0, 0, 0)),
        ],
        out_specs=[big, pl.BlockSpec((WIDE, 1, BLOCK), lambda b: (b, 0, 0))],
        out_shape=[
            pltpu.VMEM((count, width), f32),
            pltpu.VMEM((nb, 1, BLOCK), f32),
        ],
        compiler_params=params(6),
        name="linear",
    )(fq, part, inner, mine, theirs, other)


def combine_body(lin_ref, win_ref, s0, s1, s2, s3, gain_ref, out_hbm, out_ref, sems):
    def send(b):
        row = pl.ds(pl.multiple_of(b * BLOCK, BLOCK), BLOCK)
        return row, pltpu.make_async_copy(out_ref.at[row], out_hbm.at[row], sems.at[b])

    @pl.loop(0, s0.shape[0])
    def _(b):
        ms = ((s0[b] + s1[b]) + (s2[b] + s3[b])) * (1.0 / (QUERY_HEADS * D))
        inv = jnp.broadcast_to(lax.rsqrt(ms + EPS), (BLOCK, BLOCK)).T
        row, copy = send(b)
        for i in range(lin_ref.shape[1] // D):
            at = slice(i * D, (i + 1) * D)
            out_ref[row, at] = lin_ref[row, at] * inv * gain_ref[:, at] + win_ref[row, at]
        copy.start()

    @pl.loop(0, s0.shape[0])
    def _(b):
        send(b)[1].wait()


def combine(lin, win, squares, gain):
    args = [lin, win, *squares, gain]
    return pl.pallas_call(
        combine_body,
        grid=(1,),
        in_specs=[pl.BlockSpec(x.shape, lambda _, x=x: (0,) * x.ndim) for x in args],
        out_specs=pl.BlockSpec(memory_space=pl.ANY),
        out_shape=pltpu.HBM(lin.shape, f32),
        scratch_shapes=[
            pltpu.VMEM(lin.shape, f32),
            pltpu.SemaphoreType.DMA((squares[0].shape[0],)),
        ],
        compiler_params=params(10),
        name="combine",
    )(*args)


def shift_x(by):
    return [(i, i // 8 * 8 + (i + 2 * by) % 8) for i in range(32)]


def down_from(y):
    return [(y * 8 + i, (y + 1) * 8 + i) for i in range(8)]


SWAP = [(i, i ^ 1) for i in range(32)]


def shards(queries, keys, values, gain):
    count = queries.shape[0]
    nb = count // BLOCK
    heads = lax.axis_size("head")
    assert heads == 4 and nb == 8 and lax.axis_size("seq") == 32
    queries, keys, values = (
        pltpu.with_memory_space_constraint(x, pltpu.HBM) for x in (queries, keys, values)
    )

    def move(x, pairs):
        return lax.ppermute(x, "seq", pairs)

    def tie(*xs):
        return lax.optimization_barrier(xs)

    order = (1, 2, 3, 0)
    inner, total, tail, kp, vp, q = local_states(queries, keys, values, order[0])
    other = move(total, SWAP)
    (chip,) = small_call(chip_body, 1, total, other)
    along_x = [move(chip, shift_x(by)) for by in (1, 2, 3)]
    halo = move(tail, [(i, i + 1) for i in range(31)])
    *made, q = block_part(order[0], q, kp, vp, (), order[1], queries)
    *made, one, two, three = tie(*made, *along_x)
    row, mine = small_call(row_body, 2, chip, one, two, three)
    for y in range(3):
        got = move(row, down_from(y))
        *made, mine = tie(*made, mine)
        if y < 2:
            *made, q = block_part(order[y + 1], q, kp, vp, made, order[y + 2], queries)
        else:
            made = block_part(0, q, kp, vp, made, halo=halo)
        *made, got = tie(*made, got)
        row, mine = row + got, mine + got
    theirs = move(mine, SWAP)
    win, part, fq = made
    lin, sq = linear_part(fq, part, inner, mine, theirs, other)
    squares = [sq]
    for by in range(1, heads):
        squares.append(lax.ppermute(sq, "head", [(i, (i + by) % heads) for i in range(heads)]))
    return combine(lin, win, squares, gain[None, :])


def solution(mesh):
    in_specs = (P("seq", "head"), P("seq", "head"), P("seq", "head"), P("head"))
    return jax.shard_map(
        shards, mesh=mesh, in_specs=in_specs, out_specs=P("seq", "head"), check_vma=False
    )
```

```python
import functools
import math

import jax
import jax.numpy as jnp
from jax import lax
from jax.experimental import pallas as pl
from jax.experimental.pallas import tpu as pltpu
from jax.sharding import PartitionSpec as P


QUERY_HEADS = 64
KEY_VALUE_HEADS = 8
D = 128
G = QUERY_HEADS // KEY_VALUE_HEADS
BLOCK = 128
STEP = 2
WIDE = 4
EPS = 1e-6
SCORE_SCALE = math.log2(math.e) / math.sqrt(D)

f32 = jnp.float32
bf = jnp.bfloat16
NT = (((1,), (1,)), ((), ()))
TN = (((0,), (0,)), ((), ()))


def split(x):
    hi = x.astype(bf)
    return hi, (x - hi.astype(f32)).astype(bf)


def lanes(*xs):
    return jnp.concatenate(xs, axis=1)


def rows(*xs):
    return jnp.concatenate(xs, axis=0)


def dot(a, b, dims=(((1,), (0,)), ((), ()))):
    return lax.dot_general(a, b, dims, preferred_element_type=f32)


def halves(x):
    return x[:, :D] + x[:, D:]


def params(mib):
    return pltpu.CompilerParams(
        vmem_limit_bytes=mib << 20, dimension_semantics=("arbitrary",)
    )


def state_body(
    k_ref, v_ref, q_hbm, before_ref, total_ref, tail_ref, kp_ref, vp_ref, q_ref, sems, *, ahead
):
    count = k_ref.shape[0]
    g = pl.program_id(0)

    def fetch(j):
        to = pl.ds(pl.multiple_of(j * BLOCK, BLOCK), BLOCK)
        at = pl.ds(pl.multiple_of((ahead * STEP + j) * BLOCK, BLOCK), BLOCK)
        return pltpu.make_async_copy(q_hbm.at[at], q_ref.at[to], sems.at[j])

    @pl.when(g == 0)
    def _():
        @pl.loop(0, STEP)
        def _(j):
            fetch(j).start()

    state = jnp.zeros((D, D), f32)
    for b in range(count // BLOCK):
        at = slice(b * BLOCK, (b + 1) * BLOCK)
        before_ref[b] = state
        k = k_ref[at, :]
        fh, fl = split(jnp.tanh(k))
        vv = lanes(*split(v_ref[at, :]))
        kp_ref[at, :] = lanes(*split(k * SCORE_SCALE), fh, fl)
        vp_ref[at, :] = vv
        state = state + halves(dot(rows(fh, fl), rows(vv, vv), TN))
    total_ref[...] = state
    tail_ref[:BLOCK] = k_ref[count - BLOCK :, :]
    tail_ref[BLOCK:] = v_ref[count - BLOCK :, :]

    @pl.when(g == pl.num_programs(0) - 1)
    def _():
        for j in range(STEP):
            fetch(j).wait()


def local_states(queries, keys, values, ahead):
    count, width = keys.shape
    kv, nb = width // D, count // BLOCK
    one = pl.Squeezed()
    whole = lambda *shape: pl.BlockSpec((one, *shape), lambda g: (g,) + (0,) * len(shape))
    q_shape = (STEP * BLOCK, queries.shape[1])
    return pl.pallas_call(
        functools.partial(state_body, ahead=ahead),
        grid=(kv,),
        in_specs=[pl.BlockSpec((count, D), lambda g: (0, g))] * 2
        + [pl.BlockSpec(memory_space=pl.ANY)],
        out_specs=[
            whole(nb, D, D),
            whole(D, D),
            whole(2 * BLOCK, D),
            whole(count, 4 * D),
            whole(count, 2 * D),
            pl.BlockSpec(memory_space=pl.ANY),
        ],
        out_shape=[
            pltpu.VMEM((kv, nb, D, D), f32),
            pltpu.VMEM((kv, D, D), f32),
            pltpu.VMEM((kv, 2 * BLOCK, D), f32),
            pltpu.VMEM((kv, count, 4 * D), bf),
            pltpu.VMEM((kv, count, 2 * D), bf),
            pltpu.VMEM(q_shape, f32),
        ],
        scratch_shapes=[pltpu.SemaphoreType.DMA((STEP,))],
        compiler_params=params(4),
        name="local_states",
    )(keys, values, queries)


def place():
    i = lax.axis_index("seq")
    return i // 8, (i // 2) % 4, i % 2


def chip_body(own_ref, other_ref, out_ref):
    core = place()[2]
    out_ref[...] = own_ref[core] + other_ref[core]


def row_body(own_ref, one_ref, two_ref, three_ref, sum_ref, before_ref):
    x = place()[1]
    got = [one_ref[...], two_ref[...], three_ref[...]]
    sum_ref[...] = own_ref[...] + got[0] + got[1] + got[2]
    before = jnp.zeros((D, D), f32)
    for by, state in enumerate(got, 1):
        before = before + jnp.where(x >= by, state, 0.0)
    before_ref[...] = before


def small_call(body, outs, *args):
    shape = jax.ShapeDtypeStruct((D, D), f32)
    return pl.pallas_call(
        body,
        out_shape=[shape] * outs,
        compiler_params=pltpu.CompilerParams(vmem_limit_bytes=2 << 20),
    )(*args)


def block_body(piece, ahead, carried, inner, window, *refs):
    q_ref, kp_ref, vp_ref, *refs = refs
    if piece == 0 and window:
        halo_ref, *refs = refs
    if ahead is not None:
        q_hbm, *refs = refs
    refs = refs[carried:]
    if window:
        win_ref, *refs = refs
    if inner:
        lin_ref, fq_ref, *refs = refs
    kv = kp_ref.shape[0]
    if ahead is not None:
        next_ref, sems = refs

        def fetch(j):
            to = pl.ds(pl.multiple_of(j * BLOCK, BLOCK), BLOCK)
            at = pl.ds(pl.multiple_of((ahead * STEP + j) * BLOCK, BLOCK), BLOCK)
            return pltpu.make_async_copy(q_hbm.at[at], next_ref.at[to], sems.at[j])

        @pl.loop(0, STEP)
        def _(j):
            fetch(j).start()

    row = lax.broadcasted_iota(jnp.int32, (BLOCK, BLOCK), 0)
    col = lax.broadcasted_iota(jnp.int32, (BLOCK, BLOCK), 1)
    own = rows(*[row >= col] * G)
    zero = jnp.zeros((BLOCK * G, BLOCK), bf)

    def in_block(j, g, q, heads, tokens, here):
        fh, fl = kp_ref[g, here, 2 * D : 3 * D], kp_ref[g, here, 3 * D :]
        v_own = vp_ref[g, here, :]
        f2 = lanes(*split(jnp.tanh(q)))
        fq_ref[j, g * G * BLOCK : (g + 1) * G * BLOCK, :] = f2
        ff = rows(lanes(fh, fh), lanes(fl, fl))
        a = jnp.where(own, halves(dot(f2, ff, NT)), 0.0)
        lin = halves(dot(lanes(*split(a)), rows(v_own, v_own)))
        for i, at in enumerate(heads):
            lin_ref[tokens, at] = lin[i * BLOCK : (i + 1) * BLOCK]

    def in_window(block, g, q, heads, tokens, here, there):
        kh, kl = kp_ref[g, here, :D], kp_ref[g, here, D : 2 * D]
        if block:
            ph, pl_ = kp_ref[g, there, :D], kp_ref[g, there, D : 2 * D]
            v_prior = vp_ref[g, there, :]
        else:
            ph, pl_ = split(halo_ref[g, :BLOCK] * SCORE_SCALE)
            v_prior = lanes(*split(halo_ref[g, BLOCK:]))
        kk = rows(lanes(kh, kh, kl, kl), lanes(ph, ph, pl_, pl_))
        v_both = rows(vp_ref[g, here, :], v_prior)
        qh, ql = split(q)
        s = dot(lanes(qh, ql, qh, ql), kk, NT)
        before = s[:, BLOCK:]
        if block == 0:
            before = jnp.where(lax.axis_index("seq") > 0, before, -1e30)
        t = jnp.where(own, s[:, :BLOCK], before)
        p = jnp.exp2(t - jnp.max(t, axis=1, keepdims=True))
        total = jnp.sum(p, axis=1, keepdims=True)
        wh, wl = split(p)
        p4 = lanes(
            jnp.where(own, wh, zero),
            jnp.where(own, zero, wh),
            jnp.where(own, wl, zero),
            jnp.where(own, zero, wl),
        )
        win = halves(dot(p4, rows(v_both, v_both))) * (1.0 / total)
        for i, at in enumerate(heads):
            win_ref[tokens, at] = win[i * BLOCK : (i + 1) * BLOCK]

    for j in range(STEP):
        block = piece * STEP + j
        tokens = slice(j * BLOCK, (j + 1) * BLOCK)
        here = slice(block * BLOCK, (block + 1) * BLOCK)
        there = slice((block - 1) * BLOCK, block * BLOCK)
        for g in range(kv):
            heads = [slice(i * D, (i + 1) * D) for i in range(g * G, (g + 1) * G)]
            q = rows(*[q_ref[tokens, at] for at in heads])
            if inner:
                in_block(j, g, q, heads, tokens, here)
            if window:
                in_window(block, g, q, heads, tokens, here, there)
    if ahead is not None:
        for j in range(STEP):
            fetch(j).wait()


def block_part(
    piece, q, kp, vp, made, ahead=None, queries=None, halo=None, inner=True, window=True
):
    kv, count, _ = kp.shape
    nb = count // BLOCK
    width = q.shape[1]
    whole = lambda x: pl.BlockSpec(x.shape, lambda _: (0,) * x.ndim)
    args = [q, kp, vp]
    if halo is not None:
        args.append(halo)
    specs = [whole(x) for x in args]
    if ahead is not None:
        args.append(queries)
        specs.append(pl.BlockSpec(memory_space=pl.ANY))
    aliases = {len(args) + i: i for i in range(len(made))}
    big = pl.BlockSpec((STEP * BLOCK, width), lambda _: (piece, 0))
    out_specs, out_shape, scratch = [], [], []
    if window:
        out_specs.append(big)
        out_shape.append(pltpu.VMEM((count, width), f32))
    if inner:
        features = (kv * G * BLOCK, 2 * D)
        out_specs += [big, pl.BlockSpec((STEP, *features), lambda _: (piece, 0, 0))]
        out_shape += [pltpu.VMEM((count, width), f32), pltpu.VMEM((nb, *features), bf)]
    if ahead is not None:
        out_specs.append(pl.BlockSpec(memory_space=pl.ANY))
        out_shape.append(pltpu.VMEM(q.shape, f32))
        scratch.append(pltpu.SemaphoreType.DMA((STEP,)))
    return pl.pallas_call(
        lambda *refs: block_body(piece, ahead, len(made), inner, window, *refs),
        grid=(1,),
        in_specs=specs + [pl.BlockSpec(memory_space=pl.ANY)] * len(made),
        out_specs=out_specs,
        out_shape=out_shape,
        scratch_shapes=scratch,
        input_output_aliases=aliases,
        compiler_params=params(10),
    )(*args, *made)


def linear_body(fq_ref, part_ref, inner_ref, mine_ref, their_ref, other_ref, lin_ref, sq_ref):
    core = place()[2]
    for j in range(WIDE):
        tokens = slice(j * BLOCK, (j + 1) * BLOCK)
        sq = jnp.zeros((BLOCK, D), f32)
        for g in range(other_ref.shape[0]):
            state = jnp.where(core == g, mine_ref[...], their_ref[...])
            state = state + jnp.where(core == 1, other_ref[g], 0.0) + inner_ref[g, j]
            ss = lanes(*split(state))
            fq = fq_ref[j, g * G * BLOCK : (g + 1) * G * BLOCK, :]
            lin = halves(dot(fq, rows(ss, ss)))
            for i in range(G):
                at = slice((g * G + i) * D, (g * G + i + 1) * D)
                x = lin[i * BLOCK : (i + 1) * BLOCK] + part_ref[tokens, at]
                lin_ref[tokens, at] = x
                sq = sq + x * x
        sq_ref[j] = jnp.sum(sq.T, axis=0, keepdims=True)


def linear_part(fq, part, inner, mine, theirs, other):
    count, width = part.shape
    kv, nb = inner.shape[:2]
    big = pl.BlockSpec((WIDE * BLOCK, width), lambda b: (b, 0))
    state = pl.BlockSpec((D, D), lambda b: (0, 0))
    return pl.pallas_call(
        linear_body,
        grid=(nb // WIDE,),
        in_specs=[
            pl.BlockSpec((WIDE,) + fq.shape[1:], lambda b: (b, 0, 0)),
            big,
            pl.BlockSpec((kv, WIDE, D, D), lambda b: (0, b, 0, 0)),
            state,
            state,
            pl.BlockSpec((kv, D, D), lambda b: (0, 0, 0)),
        ],
        out_specs=[big, pl.BlockSpec((WIDE, 1, BLOCK), lambda b: (b, 0, 0))],
        out_shape=[
            pltpu.VMEM((count, width), f32),
            pltpu.VMEM((nb, 1, BLOCK), f32),
        ],
        compiler_params=params(10),
        name="linear",
    )(fq, part, inner, mine, theirs, other)


def combine_body(lin_ref, win_ref, s0, s1, s2, s3, gain_ref, out_hbm, out_ref, sems):
    def send(b):
        row = pl.ds(pl.multiple_of(b * BLOCK, BLOCK), BLOCK)
        return row, pltpu.make_async_copy(out_ref.at[row], out_hbm.at[row], sems.at[b])

    @pl.loop(0, s0.shape[0])
    def _(b):
        ms = ((s0[b] + s1[b]) + (s2[b] + s3[b])) * (1.0 / (QUERY_HEADS * D))
        inv = jnp.broadcast_to(lax.rsqrt(ms + EPS), (BLOCK, BLOCK)).T
        row, copy = send(b)
        for i in range(lin_ref.shape[1] // D):
            at = slice(i * D, (i + 1) * D)
            out_ref[row, at] = lin_ref[row, at] * inv * gain_ref[:, at] + win_ref[row, at]
        copy.start()

    @pl.loop(0, s0.shape[0])
    def _(b):
        send(b)[1].wait()


def combine(lin, win, squares, gain):
    args = [lin, win, *squares, gain]
    return pl.pallas_call(
        combine_body,
        grid=(1,),
        in_specs=[pl.BlockSpec(x.shape, lambda _, x=x: (0,) * x.ndim) for x in args],
        out_specs=pl.BlockSpec(memory_space=pl.ANY),
        out_shape=pltpu.HBM(lin.shape, f32),
        scratch_shapes=[
            pltpu.VMEM(lin.shape, f32),
            pltpu.SemaphoreType.DMA((squares[0].shape[0],)),
        ],
        compiler_params=params(10),
        name="combine",
    )(*args)


def shift_x(by):
    return [(i, i // 8 * 8 + (i + 2 * by) % 8) for i in range(32)]


def down_from(y):
    return [(y * 8 + i, (y + 1) * 8 + i) for i in range(8)]


SWAP = [(i, i ^ 1) for i in range(32)]


def shards(queries, keys, values, gain):
    count = queries.shape[0]
    nb = count // BLOCK
    heads = lax.axis_size("head")
    assert heads == 4 and nb == 8 and lax.axis_size("seq") == 32
    queries, keys, values = (
        pltpu.with_memory_space_constraint(x, pltpu.HBM) for x in (queries, keys, values)
    )

    def move(x, pairs):
        return lax.ppermute(x, "seq", pairs)

    def tie(*xs):
        return lax.optimization_barrier(xs)

    order = (1, 2, 3, 0)
    inner, total, tail, kp, vp, q = local_states(queries, keys, values, order[0])
    other = move(total, SWAP)
    (chip,) = small_call(chip_body, 1, total, other)
    along_x = [move(chip, shift_x(by)) for by in (1, 2, 3)]
    halo = move(tail, [(i, i + 1) for i in range(31)])
    *made, q = block_part(order[0], q, kp, vp, (), order[1], queries)
    *made, one, two, three = tie(*made, *along_x)
    row, mine = small_call(row_body, 2, chip, one, two, three)
    for y in range(3):
        got = move(row, down_from(y))
        *made, mine = tie(*made, mine)
        if y < 2:
            *made, q = block_part(order[y + 1], q, kp, vp, made, order[y + 2], queries)
        else:
            win, *made = made
            part, fq = block_part(0, q, kp, vp, made, window=False)
            made = [win, part, fq]
        *made, got = tie(*made, got)
        row, mine = row + got, mine + got
    theirs = move(mine, SWAP)
    win, part, fq = made
    lin, sq = linear_part(fq, part, inner, mine, theirs, other)
    q, sq = tie(q, sq)
    squares = [sq]
    for by in range(1, heads):
        squares.append(lax.ppermute(sq, "head", [(i, (i + by) % heads) for i in range(heads)]))
    (win,) = block_part(0, q, kp, vp, (win,), halo=halo, inner=False)
    return combine(lin, win, squares, gain[None, :])


def solution(mesh):
    in_specs = (P("seq", "head"), P("seq", "head"), P("seq", "head"), P("head"))
    return jax.shard_map(
        shards, mesh=mesh, in_specs=in_specs, out_specs=P("seq", "head"), check_vma=False
    )
```

```python
import functools
import math

import jax
import jax.numpy as jnp
from jax import lax
from jax.experimental import pallas as pl
from jax.experimental.pallas import tpu as pltpu
from jax.sharding import PartitionSpec as P


QUERY_HEADS = 64
KEY_VALUE_HEADS = 8
D = 128
G = QUERY_HEADS // KEY_VALUE_HEADS
BLOCK = 128
STEP = 2
WIDE = 4
EPS = 1e-6
SCORE_SCALE = math.log2(math.e) / math.sqrt(D)

f32 = jnp.float32
bf = jnp.bfloat16
NT = (((1,), (1,)), ((), ()))
TN = (((0,), (0,)), ((), ()))


def split(x):
    hi = x.astype(bf)
    return hi, (x - hi.astype(f32)).astype(bf)


def lanes(*xs):
    return jnp.concatenate(xs, axis=1)


def rows(*xs):
    return jnp.concatenate(xs, axis=0)


def dot(a, b, dims=(((1,), (0,)), ((), ()))):
    return lax.dot_general(a, b, dims, preferred_element_type=f32)


def halves(x):
    return x[:, :D] + x[:, D:]


def params(mib):
    return pltpu.CompilerParams(
        vmem_limit_bytes=mib << 20, dimension_semantics=("arbitrary",)
    )


def state_body(k_ref, v_ref, before_ref, total_ref, tail_ref, kp_ref, vp_ref):
    count = k_ref.shape[0]
    state = jnp.zeros((D, D), f32)
    for b in range(count // BLOCK):
        at = slice(b * BLOCK, (b + 1) * BLOCK)
        before_ref[b] = state
        k = k_ref[at, :]
        fh, fl = split(jnp.tanh(k))
        vv = lanes(*split(v_ref[at, :]))
        kp_ref[at, :] = lanes(*split(k * SCORE_SCALE), fh, fl)
        vp_ref[at, :] = vv
        state = state + halves(dot(rows(fh, fl), rows(vv, vv), TN))
    total_ref[...] = state
    tail_ref[:BLOCK] = k_ref[count - BLOCK :, :]
    tail_ref[BLOCK:] = v_ref[count - BLOCK :, :]


def local_states(keys, values):
    count, width = keys.shape
    kv, nb = width // D, count // BLOCK
    one = pl.Squeezed()
    whole = lambda *shape: pl.BlockSpec((one, *shape), lambda g: (g,) + (0,) * len(shape))
    return pl.pallas_call(
        state_body,
        grid=(kv,),
        in_specs=[pl.BlockSpec((count, D), lambda g: (0, g))] * 2,
        out_specs=[
            whole(nb, D, D),
            whole(D, D),
            whole(2 * BLOCK, D),
            whole(count, 4 * D),
            whole(count, 2 * D),
        ],
        out_shape=[
            pltpu.VMEM((kv, nb, D, D), f32),
            pltpu.VMEM((kv, D, D), f32),
            pltpu.VMEM((kv, 2 * BLOCK, D), f32),
            pltpu.VMEM((kv, count, 4 * D), bf),
            pltpu.VMEM((kv, count, 2 * D), bf),
        ],
        compiler_params=params(4),
        name="local_states",
    )(keys, values)


def block_copy(piece, q_hbm, q_ref, sems, j):
    to = pl.ds(pl.multiple_of(j * BLOCK, BLOCK), BLOCK)
    at = pl.ds(pl.multiple_of((piece * STEP + j) * BLOCK, BLOCK), BLOCK)
    return pltpu.make_async_copy(q_hbm.at[at], q_ref.at[to], sems.at[j])


def fetch_body(piece, *refs):
    for j in range(STEP):
        block_copy(piece, *refs, j).start()
    for j in range(STEP):
        block_copy(piece, *refs, j).wait()


def first_queries(queries, piece):
    return pl.pallas_call(
        functools.partial(fetch_body, piece),
        in_specs=[pl.BlockSpec(memory_space=pl.ANY)],
        out_specs=pl.BlockSpec(memory_space=pl.ANY),
        out_shape=pltpu.VMEM((STEP * BLOCK, queries.shape[1]), f32),
        scratch_shapes=[pltpu.SemaphoreType.DMA((STEP,))],
        compiler_params=pltpu.CompilerParams(vmem_limit_bytes=2 << 20),
        name="first_queries",
    )(queries)


def place():
    i = lax.axis_index("seq")
    return i // 8, (i // 2) % 4, i % 2


def chip_body(own_ref, other_ref, out_ref):
    core = place()[2]
    out_ref[...] = own_ref[core] + other_ref[core]


def row_body(own_ref, one_ref, two_ref, three_ref, sum_ref, before_ref):
    x = place()[1]
    got = [one_ref[...], two_ref[...], three_ref[...]]
    sum_ref[...] = own_ref[...] + got[0] + got[1] + got[2]
    before = jnp.zeros((D, D), f32)
    for by, state in enumerate(got, 1):
        before = before + jnp.where(x >= by, state, 0.0)
    before_ref[...] = before


def small_call(body, outs, *args):
    shape = jax.ShapeDtypeStruct((D, D), f32)
    return pl.pallas_call(
        body,
        out_shape=[shape] * outs,
        compiler_params=pltpu.CompilerParams(vmem_limit_bytes=2 << 20),
    )(*args)


def block_body(piece, ahead, carried, inner, window, *refs):
    q_ref, kp_ref, vp_ref, *refs = refs
    if piece == 0 and window:
        halo_ref, *refs = refs
    if ahead is not None:
        q_hbm, *refs = refs
    refs = refs[carried:]
    if window:
        win_ref, *refs = refs
    if inner:
        lin_ref, fq_ref, *refs = refs
    kv = kp_ref.shape[0]
    if ahead is not None:
        next_ref, sems = refs
        fetch = functools.partial(block_copy, ahead, q_hbm, next_ref, sems)

        @pl.loop(0, STEP)
        def _(j):
            fetch(j).start()

    row = lax.broadcasted_iota(jnp.int32, (BLOCK, BLOCK), 0)
    col = lax.broadcasted_iota(jnp.int32, (BLOCK, BLOCK), 1)
    own = rows(*[row >= col] * G)
    zero = jnp.zeros((BLOCK * G, BLOCK), bf)

    def in_block(j, g, q, heads, tokens, here):
        fh, fl = kp_ref[g, here, 2 * D : 3 * D], kp_ref[g, here, 3 * D :]
        v_own = vp_ref[g, here, :]
        f2 = lanes(*split(jnp.tanh(q)))
        fq_ref[j, g * G * BLOCK : (g + 1) * G * BLOCK, :] = f2
        ff = rows(lanes(fh, fh), lanes(fl, fl))
        a = jnp.where(own, halves(dot(f2, ff, NT)), 0.0)
        lin = halves(dot(lanes(*split(a)), rows(v_own, v_own)))
        for i, at in enumerate(heads):
            lin_ref[tokens, at] = lin[i * BLOCK : (i + 1) * BLOCK]

    def scores(block, g, q, here, there):
        kh, kl = kp_ref[g, here, :D], kp_ref[g, here, D : 2 * D]
        if block:
            ph, pl_ = kp_ref[g, there, :D], kp_ref[g, there, D : 2 * D]
            v_prior = vp_ref[g, there, :]
        else:
            ph, pl_ = split(halo_ref[g, :BLOCK] * SCORE_SCALE)
            v_prior = lanes(*split(halo_ref[g, BLOCK:]))
        kk = rows(lanes(kh, kh, kl, kl), lanes(ph, ph, pl_, pl_))
        v_both = rows(vp_ref[g, here, :], v_prior)
        qh, ql = split(q)
        return dot(lanes(qh, ql, qh, ql), kk, NT), v_both

    def in_window(block, s, v_both, heads, tokens):
        before = s[:, BLOCK:]
        if block == 0:
            before = jnp.where(lax.axis_index("seq") > 0, before, -1e30)
        t = jnp.where(own, s[:, :BLOCK], before)
        p = jnp.exp2(t - jnp.max(t, axis=1, keepdims=True))
        total = jnp.sum(p, axis=1, keepdims=True)
        wh, wl = split(p)
        p4 = lanes(
            jnp.where(own, wh, zero),
            jnp.where(own, zero, wh),
            jnp.where(own, wl, zero),
            jnp.where(own, zero, wl),
        )
        win = halves(dot(p4, rows(v_both, v_both))) * (1.0 / total)
        for i, at in enumerate(heads):
            win_ref[tokens, at] = win[i * BLOCK : (i + 1) * BLOCK]

    for j in range(STEP):
        block = piece * STEP + j
        tokens = slice(j * BLOCK, (j + 1) * BLOCK)
        here = slice(block * BLOCK, (block + 1) * BLOCK)
        there = slice((block - 1) * BLOCK, block * BLOCK)
        for g in range(kv):
            heads = [slice(i * D, (i + 1) * D) for i in range(g * G, (g + 1) * G)]
            q = rows(*[q_ref[tokens, at] for at in heads])
            if window:
                s, v_both = scores(block, g, q, here, there)
            if inner:
                in_block(j, g, q, heads, tokens, here)
            if window:
                in_window(block, s, v_both, heads, tokens)
    if ahead is not None:
        for j in range(STEP):
            fetch(j).wait()


def block_part(
    piece, q, kp, vp, made, ahead=None, queries=None, halo=None, inner=True, window=True
):
    kv, count, _ = kp.shape
    nb = count // BLOCK
    width = q.shape[1]
    whole = lambda x: pl.BlockSpec(x.shape, lambda _: (0,) * x.ndim)
    args = [q, kp, vp]
    if halo is not None:
        args.append(halo)
    specs = [whole(x) for x in args]
    if ahead is not None:
        args.append(queries)
        specs.append(pl.BlockSpec(memory_space=pl.ANY))
    aliases = {len(args) + i: i for i in range(len(made))}
    big = pl.BlockSpec((STEP * BLOCK, width), lambda _: (piece, 0))
    out_specs, out_shape, scratch = [], [], []
    if window:
        out_specs.append(big)
        out_shape.append(pltpu.VMEM((count, width), f32))
    if inner:
        features = (kv * G * BLOCK, 2 * D)
        out_specs += [big, pl.BlockSpec((STEP, *features), lambda _: (piece, 0, 0))]
        out_shape += [pltpu.VMEM((count, width), f32), pltpu.VMEM((nb, *features), bf)]
    if ahead is not None:
        out_specs.append(pl.BlockSpec(memory_space=pl.ANY))
        out_shape.append(pltpu.VMEM(q.shape, f32))
        scratch.append(pltpu.SemaphoreType.DMA((STEP,)))
    return pl.pallas_call(
        lambda *refs: block_body(piece, ahead, len(made), inner, window, *refs),
        grid=(1,),
        in_specs=specs + [pl.BlockSpec(memory_space=pl.ANY)] * len(made),
        out_specs=out_specs,
        out_shape=out_shape,
        scratch_shapes=scratch,
        input_output_aliases=aliases,
        compiler_params=params(10),
    )(*args, *made)


def linear_body(fq_ref, part_ref, inner_ref, mine_ref, their_ref, other_ref, lin_ref, sq_ref):
    core = place()[2]
    for j in range(WIDE):
        tokens = slice(j * BLOCK, (j + 1) * BLOCK)
        sq = jnp.zeros((BLOCK, D), f32)
        for g in range(other_ref.shape[0]):
            state = jnp.where(core == g, mine_ref[...], their_ref[...])
            state = state + jnp.where(core == 1, other_ref[g], 0.0) + inner_ref[g, j]
            ss = lanes(*split(state))
            fq = fq_ref[j, g * G * BLOCK : (g + 1) * G * BLOCK, :]
            lin = halves(dot(fq, rows(ss, ss)))
            for i in range(G):
                at = slice((g * G + i) * D, (g * G + i + 1) * D)
                x = lin[i * BLOCK : (i + 1) * BLOCK] + part_ref[tokens, at]
                lin_ref[tokens, at] = x
                sq = sq + x * x
        sq_ref[j] = jnp.sum(sq.T, axis=0, keepdims=True)


def linear_part(fq, part, inner, mine, theirs, other):
    count, width = part.shape
    kv, nb = inner.shape[:2]
    big = pl.BlockSpec((WIDE * BLOCK, width), lambda b: (b, 0))
    state = pl.BlockSpec((D, D), lambda b: (0, 0))
    return pl.pallas_call(
        linear_body,
        grid=(nb // WIDE,),
        in_specs=[
            pl.BlockSpec((WIDE,) + fq.shape[1:], lambda b: (b, 0, 0)),
            big,
            pl.BlockSpec((kv, WIDE, D, D), lambda b: (0, b, 0, 0)),
            state,
            state,
            pl.BlockSpec((kv, D, D), lambda b: (0, 0, 0)),
        ],
        out_specs=[big, pl.BlockSpec((WIDE, 1, BLOCK), lambda b: (b, 0, 0))],
        out_shape=[
            pltpu.VMEM((count, width), f32),
            pltpu.VMEM((nb, 1, BLOCK), f32),
        ],
        compiler_params=params(10),
        name="linear",
    )(fq, part, inner, mine, theirs, other)


def combine_body(lin_ref, win_ref, s0, s1, s2, s3, gain_ref, out_hbm, out_ref, sems):
    def send(b):
        row = pl.ds(pl.multiple_of(b * BLOCK, BLOCK), BLOCK)
        return row, pltpu.make_async_copy(out_ref.at[row], out_hbm.at[row], sems.at[b])

    @pl.loop(0, s0.shape[0])
    def _(b):
        ms = ((s0[b] + s1[b]) + (s2[b] + s3[b])) * (1.0 / (QUERY_HEADS * D))
        inv = jnp.broadcast_to(lax.rsqrt(ms + EPS), (BLOCK, BLOCK)).T
        row, copy = send(b)
        for i in range(lin_ref.shape[1] // D):
            at = slice(i * D, (i + 1) * D)
            out_ref[row, at] = lin_ref[row, at] * inv * gain_ref[:, at] + win_ref[row, at]
        copy.start()

    @pl.loop(0, s0.shape[0])
    def _(b):
        send(b)[1].wait()


def combine(lin, win, squares, gain):
    args = [lin, win, *squares, gain]
    return pl.pallas_call(
        combine_body,
        grid=(1,),
        in_specs=[pl.BlockSpec(x.shape, lambda _, x=x: (0,) * x.ndim) for x in args],
        out_specs=pl.BlockSpec(memory_space=pl.ANY),
        out_shape=pltpu.HBM(lin.shape, f32),
        scratch_shapes=[
            pltpu.VMEM(lin.shape, f32),
            pltpu.SemaphoreType.DMA((squares[0].shape[0],)),
        ],
        compiler_params=params(10),
        name="combine",
    )(*args)


def shift_x(by):
    return [(i, i // 8 * 8 + (i + 2 * by) % 8) for i in range(32)]


def down_from(y):
    return [(y * 8 + i, (y + 1) * 8 + i) for i in range(8)]


SWAP = [(i, i ^ 1) for i in range(32)]


def shards(queries, keys, values, gain):
    count = queries.shape[0]
    nb = count // BLOCK
    heads = lax.axis_size("head")
    assert heads == 4 and nb == 8 and lax.axis_size("seq") == 32
    queries, keys, values = (
        pltpu.with_memory_space_constraint(x, pltpu.HBM) for x in (queries, keys, values)
    )

    def move(x, pairs):
        return lax.ppermute(x, "seq", pairs)

    def tie(*xs):
        return lax.optimization_barrier(xs)

    order = (1, 2, 3, 0)
    inner, total, tail, kp, vp = local_states(keys, values)
    other = move(total, SWAP)
    q = first_queries(queries, order[0])
    (chip,) = small_call(chip_body, 1, total, other)
    along_x = [move(chip, shift_x(by)) for by in (1, 2, 3)]
    *made, q = block_part(order[0], q, kp, vp, (), order[1], queries)
    *made, one, two, three = tie(*made, *along_x)
    row, mine = small_call(row_body, 2, chip, one, two, three)
    for y in range(3):
        got = move(row, down_from(y))
        *made, mine = tie(*made, mine)
        if y < 2:
            *made, q = block_part(order[y + 1], q, kp, vp, made, order[y + 2], queries)
        else:
            win, *made = made
            part, fq = block_part(0, q, kp, vp, made, window=False)
            made = [win, part, fq]
        *made, got = tie(*made, got)
        row, mine = row + got, mine + got
    tail, mine = tie(tail, mine)
    theirs = move(mine, SWAP)
    halo = move(tail, [(i, i + 1) for i in range(31)])
    win, part, fq = made
    lin, sq = linear_part(fq, part, inner, mine, theirs, other)
    q, sq = tie(q, sq)
    squares = [sq]
    for by in range(1, heads):
        squares.append(lax.ppermute(sq, "head", [(i, (i + by) % heads) for i in range(heads)]))
    (win,) = block_part(0, q, kp, vp, (win,), halo=halo, inner=False)
    return combine(lin, win, squares, gain[None, :])


def solution(mesh):
    in_specs = (P("seq", "head"), P("seq", "head"), P("seq", "head"), P("head"))
    return jax.shard_map(
        shards, mesh=mesh, in_specs=in_specs, out_specs=P("seq", "head"), check_vma=False
    )
```

```python
import functools
import math

import jax
import jax.numpy as jnp
from jax import lax
from jax.experimental import pallas as pl
from jax.experimental.pallas import tpu as pltpu
from jax.sharding import PartitionSpec as P


QUERY_HEADS = 64
KEY_VALUE_HEADS = 8
D = 128
G = QUERY_HEADS // KEY_VALUE_HEADS
BLOCK = 128
STEP = 2
WIDE = 8
EPS = 1e-6
SCORE_SCALE = math.log2(math.e) / math.sqrt(D)

f32 = jnp.float32
bf = jnp.bfloat16
NT = (((1,), (1,)), ((), ()))
TN = (((0,), (0,)), ((), ()))


def split(x):
    hi = x.astype(bf)
    return hi, (x - hi.astype(f32)).astype(bf)


def lanes(*xs):
    return jnp.concatenate(xs, axis=1)


def rows(*xs):
    return jnp.concatenate(xs, axis=0)


def dot(a, b, dims=(((1,), (0,)), ((), ()))):
    return lax.dot_general(a, b, dims, preferred_element_type=f32)


def halves(x):
    return x[:, :D] + x[:, D:]


def params(mib):
    return pltpu.CompilerParams(
        vmem_limit_bytes=mib << 20, dimension_semantics=("arbitrary",)
    )


def state_body(k_ref, v_ref, before_ref, total_ref, tail_ref, kp_ref, vp_ref):
    count = k_ref.shape[0]
    state = jnp.zeros((D, D), f32)
    for b in range(count // BLOCK):
        at = slice(b * BLOCK, (b + 1) * BLOCK)
        before_ref[b] = state
        k = k_ref[at, :]
        fh, fl = split(jnp.tanh(k))
        vv = lanes(*split(v_ref[at, :]))
        kp_ref[at, :] = lanes(*split(k * SCORE_SCALE), fh, fl)
        vp_ref[at, :] = vv
        state = state + halves(dot(rows(fh, fl), rows(vv, vv), TN))
    total_ref[...] = state
    tail_ref[:BLOCK] = k_ref[count - BLOCK :, :]
    tail_ref[BLOCK:] = v_ref[count - BLOCK :, :]


def local_states(keys, values):
    count, width = keys.shape
    kv, nb = width // D, count // BLOCK
    one = pl.Squeezed()
    whole = lambda *shape: pl.BlockSpec((one, *shape), lambda g: (g,) + (0,) * len(shape))
    return pl.pallas_call(
        state_body,
        grid=(kv,),
        in_specs=[pl.BlockSpec((count, D), lambda g: (0, g))] * 2,
        out_specs=[
            whole(nb, D, D),
            whole(D, D),
            whole(2 * BLOCK, D),
            whole(count, 4 * D),
            whole(count, 2 * D),
        ],
        out_shape=[
            pltpu.VMEM((kv, nb, D, D), f32),
            pltpu.VMEM((kv, D, D), f32),
            pltpu.VMEM((kv, 2 * BLOCK, D), f32),
            pltpu.VMEM((kv, count, 4 * D), bf),
            pltpu.VMEM((kv, count, 2 * D), bf),
        ],
        compiler_params=params(4),
        name="local_states",
    )(keys, values)


def block_copy(piece, q_hbm, q_ref, sems, j):
    to = pl.ds(pl.multiple_of(j * BLOCK, BLOCK), BLOCK)
    at = pl.ds(pl.multiple_of((piece * STEP + j) * BLOCK, BLOCK), BLOCK)
    return pltpu.make_async_copy(q_hbm.at[at], q_ref.at[to], sems.at[j])


def fetch_body(piece, *refs):
    for j in range(STEP):
        block_copy(piece, *refs, j).start()
    for j in range(STEP):
        block_copy(piece, *refs, j).wait()


def first_queries(queries, piece):
    return pl.pallas_call(
        functools.partial(fetch_body, piece),
        in_specs=[pl.BlockSpec(memory_space=pl.ANY)],
        out_specs=pl.BlockSpec(memory_space=pl.ANY),
        out_shape=pltpu.VMEM((STEP * BLOCK, queries.shape[1]), f32),
        scratch_shapes=[pltpu.SemaphoreType.DMA((STEP,))],
        compiler_params=pltpu.CompilerParams(vmem_limit_bytes=2 << 20),
        name="first_queries",
    )(queries)


def place():
    i = lax.axis_index("seq")
    return i // 8, (i // 2) % 4, i % 2


def chip_body(own_ref, other_ref, out_ref):
    core = place()[2]
    out_ref[...] = own_ref[core] + other_ref[core]


def row_body(own_ref, one_ref, two_ref, three_ref, sum_ref, before_ref):
    x = place()[1]
    got = [one_ref[...], two_ref[...], three_ref[...]]
    sum_ref[...] = own_ref[...] + got[0] + got[1] + got[2]
    before = jnp.zeros((D, D), f32)
    for by, state in enumerate(got, 1):
        before = before + jnp.where(x >= by, state, 0.0)
    before_ref[...] = before


def small_call(body, outs, *args):
    shape = jax.ShapeDtypeStruct((D, D), f32)
    return pl.pallas_call(
        body,
        out_shape=[shape] * outs,
        compiler_params=pltpu.CompilerParams(vmem_limit_bytes=2 << 20),
    )(*args)


def block_body(piece, ahead, carried, inner, window, *refs):
    q_ref, kp_ref, vp_ref, *refs = refs
    if piece == 0 and window:
        halo_ref, *refs = refs
    if ahead is not None:
        q_hbm, *refs = refs
    refs = refs[carried:]
    if window:
        win_ref, *refs = refs
    if inner:
        lin_ref, fq_ref, *refs = refs
    kv = kp_ref.shape[0]
    if ahead is not None:
        next_ref, sems = refs
        fetch = functools.partial(block_copy, ahead, q_hbm, next_ref, sems)

        @pl.loop(0, STEP)
        def _(j):
            fetch(j).start()

    row = lax.broadcasted_iota(jnp.int32, (BLOCK, BLOCK), 0)
    col = lax.broadcasted_iota(jnp.int32, (BLOCK, BLOCK), 1)
    own = rows(*[row >= col] * G)
    zero = jnp.zeros((BLOCK * G, BLOCK), bf)

    def in_block(j, g, q, heads, tokens, here):
        fh, fl = kp_ref[g, here, 2 * D : 3 * D], kp_ref[g, here, 3 * D :]
        v_own = vp_ref[g, here, :]
        f2 = lanes(*split(jnp.tanh(q)))
        fq_ref[j, g * G * BLOCK : (g + 1) * G * BLOCK, :] = f2
        ff = rows(lanes(fh, fh), lanes(fl, fl))
        a = jnp.where(own, halves(dot(f2, ff, NT)), 0.0)
        lin = halves(dot(lanes(*split(a)), rows(v_own, v_own)))
        for i, at in enumerate(heads):
            lin_ref[tokens, at] = lin[i * BLOCK : (i + 1) * BLOCK]

    def scores(block, g, q, here, there):
        kh, kl = kp_ref[g, here, :D], kp_ref[g, here, D : 2 * D]
        if block:
            ph, pl_ = kp_ref[g, there, :D], kp_ref[g, there, D : 2 * D]
            v_prior = vp_ref[g, there, :]
        else:
            ph, pl_ = split(halo_ref[g, :BLOCK] * SCORE_SCALE)
            v_prior = lanes(*split(halo_ref[g, BLOCK:]))
        kk = rows(lanes(kh, kh, kl, kl), lanes(ph, ph, pl_, pl_))
        v_both = rows(vp_ref[g, here, :], v_prior)
        qh, ql = split(q)
        return dot(lanes(qh, ql, qh, ql), kk, NT), v_both

    def in_window(block, s, v_both, heads, tokens):
        before = s[:, BLOCK:]
        if block == 0:
            before = jnp.where(lax.axis_index("seq") > 0, before, -1e30)
        t = jnp.where(own, s[:, :BLOCK], before)
        p = jnp.exp2(t - jnp.max(t, axis=1, keepdims=True))
        total = jnp.sum(p, axis=1, keepdims=True)
        wh, wl = split(p)
        p4 = lanes(
            jnp.where(own, wh, zero),
            jnp.where(own, zero, wh),
            jnp.where(own, wl, zero),
            jnp.where(own, zero, wl),
        )
        win = halves(dot(p4, rows(v_both, v_both))) * (1.0 / total)
        for i, at in enumerate(heads):
            win_ref[tokens, at] = win[i * BLOCK : (i + 1) * BLOCK]

    waiting = None
    for j in range(STEP):
        block = piece * STEP + j
        tokens = slice(j * BLOCK, (j + 1) * BLOCK)
        here = slice(block * BLOCK, (block + 1) * BLOCK)
        there = slice((block - 1) * BLOCK, block * BLOCK)
        for g in range(kv):
            heads = [slice(i * D, (i + 1) * D) for i in range(g * G, (g + 1) * G)]
            q = rows(*[q_ref[tokens, at] for at in heads])
            if window:
                made = (block, *scores(block, g, q, here, there), heads, tokens)
            if inner:
                in_block(j, g, q, heads, tokens, here)
                if window:
                    in_window(*made)
            else:
                if waiting is not None:
                    in_window(*waiting)
                waiting = made
    if waiting is not None:
        in_window(*waiting)
    if ahead is not None:
        for j in range(STEP):
            fetch(j).wait()


def block_part(
    piece, q, kp, vp, made, ahead=None, queries=None, halo=None, inner=True, window=True
):
    kv, count, _ = kp.shape
    nb = count // BLOCK
    width = q.shape[1]
    whole = lambda x: pl.BlockSpec(x.shape, lambda _: (0,) * x.ndim)
    args = [q, kp, vp]
    if halo is not None:
        args.append(halo)
    specs = [whole(x) for x in args]
    if ahead is not None:
        args.append(queries)
        specs.append(pl.BlockSpec(memory_space=pl.ANY))
    aliases = {len(args) + i: i for i in range(len(made))}
    big = pl.BlockSpec((STEP * BLOCK, width), lambda _: (piece, 0))
    out_specs, out_shape, scratch = [], [], []
    if window:
        out_specs.append(big)
        out_shape.append(pltpu.VMEM((count, width), f32))
    if inner:
        features = (kv * G * BLOCK, 2 * D)
        out_specs += [big, pl.BlockSpec((STEP, *features), lambda _: (piece, 0, 0))]
        out_shape += [pltpu.VMEM((count, width), f32), pltpu.VMEM((nb, *features), bf)]
    if ahead is not None:
        out_specs.append(pl.BlockSpec(memory_space=pl.ANY))
        out_shape.append(pltpu.VMEM(q.shape, f32))
        scratch.append(pltpu.SemaphoreType.DMA((STEP,)))
    return pl.pallas_call(
        lambda *refs: block_body(piece, ahead, len(made), inner, window, *refs),
        grid=(1,),
        in_specs=specs + [pl.BlockSpec(memory_space=pl.ANY)] * len(made),
        out_specs=out_specs,
        out_shape=out_shape,
        scratch_shapes=scratch,
        input_output_aliases=aliases,
        compiler_params=params(10),
    )(*args, *made)


def linear_body(fq_ref, part_ref, inner_ref, mine_ref, their_ref, other_ref, lin_ref, sq_ref):
    core = place()[2]
    for j in range(WIDE):
        tokens = slice(j * BLOCK, (j + 1) * BLOCK)
        sq = jnp.zeros((BLOCK, D), f32)
        for g in range(other_ref.shape[0]):
            state = jnp.where(core == g, mine_ref[...], their_ref[...])
            state = state + jnp.where(core == 1, other_ref[g], 0.0) + inner_ref[g, j]
            ss = lanes(*split(state))
            fq = fq_ref[j, g * G * BLOCK : (g + 1) * G * BLOCK, :]
            lin = halves(dot(fq, rows(ss, ss)))
            for i in range(G):
                at = slice((g * G + i) * D, (g * G + i + 1) * D)
                x = lin[i * BLOCK : (i + 1) * BLOCK] + part_ref[tokens, at]
                lin_ref[tokens, at] = x
                sq = sq + x * x
        sq_ref[j] = jnp.sum(sq.T, axis=0, keepdims=True)


def linear_part(fq, part, inner, mine, theirs, other):
    count, width = part.shape
    kv, nb = inner.shape[:2]
    big = pl.BlockSpec((WIDE * BLOCK, width), lambda b: (b, 0))
    state = pl.BlockSpec((D, D), lambda b: (0, 0))
    return pl.pallas_call(
        linear_body,
        grid=(nb // WIDE,),
        in_specs=[
            pl.BlockSpec((WIDE,) + fq.shape[1:], lambda b: (b, 0, 0)),
            big,
            pl.BlockSpec((kv, WIDE, D, D), lambda b: (0, b, 0, 0)),
            state,
            state,
            pl.BlockSpec((kv, D, D), lambda b: (0, 0, 0)),
        ],
        out_specs=[big, pl.BlockSpec((WIDE, 1, BLOCK), lambda b: (b, 0, 0))],
        out_shape=[
            pltpu.VMEM((count, width), f32),
            pltpu.VMEM((nb, 1, BLOCK), f32),
        ],
        compiler_params=params(10),
        name="linear",
    )(fq, part, inner, mine, theirs, other)


def combine_body(lin_ref, win_ref, s0, s1, s2, s3, gain_ref, out_hbm, out_ref, sems):
    def send(b):
        row = pl.ds(pl.multiple_of(b * BLOCK, BLOCK), BLOCK)
        return row, pltpu.make_async_copy(out_ref.at[row], out_hbm.at[row], sems.at[b])

    @pl.loop(0, s0.shape[0])
    def _(b):
        ms = ((s0[b] + s1[b]) + (s2[b] + s3[b])) * (1.0 / (QUERY_HEADS * D))
        inv = jnp.broadcast_to(lax.rsqrt(ms + EPS), (BLOCK, BLOCK)).T
        row, copy = send(b)
        for i in range(lin_ref.shape[1] // D):
            at = slice(i * D, (i + 1) * D)
            out_ref[row, at] = lin_ref[row, at] * inv * gain_ref[:, at] + win_ref[row, at]
        copy.start()

    @pl.loop(0, s0.shape[0])
    def _(b):
        send(b)[1].wait()


def combine(lin, win, squares, gain):
    args = [lin, win, *squares, gain]
    return pl.pallas_call(
        combine_body,
        grid=(1,),
        in_specs=[pl.BlockSpec(x.shape, lambda _, x=x: (0,) * x.ndim) for x in args],
        out_specs=pl.BlockSpec(memory_space=pl.ANY),
        out_shape=pltpu.HBM(lin.shape, f32),
        scratch_shapes=[
            pltpu.VMEM(lin.shape, f32),
            pltpu.SemaphoreType.DMA((squares[0].shape[0],)),
        ],
        compiler_params=params(10),
        name="combine",
    )(*args)


def shift_x(by):
    return [(i, i // 8 * 8 + (i + 2 * by) % 8) for i in range(32)]


def down_from(y):
    return [(y * 8 + i, (y + 1) * 8 + i) for i in range(8)]


SWAP = [(i, i ^ 1) for i in range(32)]


def shards(queries, keys, values, gain):
    count = queries.shape[0]
    nb = count // BLOCK
    heads = lax.axis_size("head")
    assert heads == 4 and nb == 8 and lax.axis_size("seq") == 32
    queries, keys, values = (
        pltpu.with_memory_space_constraint(x, pltpu.HBM) for x in (queries, keys, values)
    )

    def move(x, pairs):
        return lax.ppermute(x, "seq", pairs)

    def tie(*xs):
        return lax.optimization_barrier(xs)

    order = (1, 2, 3, 0)
    inner, total, tail, kp, vp = local_states(keys, values)
    other = move(total, SWAP)
    q = first_queries(queries, order[0])
    (chip,) = small_call(chip_body, 1, total, other)
    along_x = [move(chip, shift_x(by)) for by in (1, 2, 3)]
    *made, q = block_part(order[0], q, kp, vp, (), order[1], queries)
    *made, one, two, three = tie(*made, *along_x)
    row, mine = small_call(row_body, 2, chip, one, two, three)
    for y in range(3):
        got = move(row, down_from(y))
        *made, mine = tie(*made, mine)
        if y < 2:
            *made, q = block_part(order[y + 1], q, kp, vp, made, order[y + 2], queries)
        else:
            win, *made = made
            part, fq = block_part(0, q, kp, vp, made, window=False)
            made = [win, part, fq]
        *made, got = tie(*made, got)
        row, mine = row + got, mine + got
    tail, mine = tie(tail, mine)
    theirs = move(mine, SWAP)
    halo = move(tail, [(i, i + 1) for i in range(31)])
    win, part, fq = made
    lin, sq = linear_part(fq, part, inner, mine, theirs, other)
    q, sq = tie(q, sq)
    squares = [sq]
    for by in range(1, heads):
        squares.append(lax.ppermute(sq, "head", [(i, (i + by) % heads) for i in range(heads)]))
    (win,) = block_part(0, q, kp, vp, (win,), halo=halo, inner=False)
    return combine(lin, win, squares, gain[None, :])


def solution(mesh):
    in_specs = (P("seq", "head"), P("seq", "head"), P("seq", "head"), P("head"))
    return jax.shard_map(
        shards, mesh=mesh, in_specs=in_specs, out_specs=P("seq", "head"), check_vma=False
    )
```
